512 devices in a mesh: space: 128 (over z, x, core), tgt: 4 (over y).
Axes of the slice: x: 4, y: 4, z: 16, core: 2. Of those that a mesh axis runs over, the one named last changes fastest.
Arguments:
- positions: float32 [2048, 3, 578], P(('space', 'tgt'))
- normals: float32 [2048, 3, 578], P(('space', 'tgt'))
- charge: float32 [2048, 578], P(('space', 'tgt')), may hold values from -6 to 6
- weights: float32 [2048, 578], P(('space', 'tgt')), may hold values from 0.5 to 2
- applied: float32 [3], replicated, may hold values from -3 to 3
- upsample: bfloat16 [578, 2112], replicated, may hold values from -0.25 to 0.25
- send_list: int32 [128, 4, 5, 4], P('space', 'tgt'), may hold values from 0 to 3, as said below
- send_count: int32 [128, 4, 5], P('space', 'tgt'), may hold values from 0 to 4, as said below
- pair_slot: int32 [128, 4, 8], P('space', 'tgt'), may hold values from 0 to 79, as said below
- pair_tile: int32 [128, 4, 8], P('space', 'tgt'), may hold values from 0 to 7
- pair_count: int32 [128, 4], P('space', 'tgt'), may hold values from 1 to 8, 16 in all within a row
Outputs:
- traction: float32 [2048, 3, 578], P(('space', 'tgt'))
- velocity: float32 [2048, 3, 578], P(('space', 'tgt'))
The draws below stay inside these ranges and needn't reach their ends.
Inputs may be any that keep to these rules, and one draw needn't show every extreme that they name: send_count is 4 at offset 2 of every device, 0 where owner index plus offset minus 2 lies outside the space axis, else 1 to 4. `send_list`: the 4 entries of one device and offset are distinct local drops. `pair_slot`: every pair, padded ones too, names a live slot of a sender inside the space axis. `pair_count`: the counts of one group along tgt sum to exactly 16, and one of them is 8.
All inputs are finite; a program needn't handle non-finite values.
Results may differ from the reference program's by a relative error of at most 0.0085.
Values may be sent and summed in bfloat16 or wider, within the bound.
No kernel may reach another device: no remote copies, remote signals or barrier semaphores. Data moves between devices by JAX's collectives and lax.ppermute only.
A program may use at most 64 MiB of HBM per device.

```python
import math
import jax
import jax.numpy as jnp
import numpy as np
from jax import lax

NC = 578
NU = 2112
DROP_DEV = 4
SLOT = 4
RANGE = 2
PAIRS = 8
GROUP_PAIRS = 16
DROPS = 2048
N_SPACE = 128
N_TGT = 4


def shell_tables(key):
    shell_size = 2 * RANGE + 1
    subkeys = jax.random.split(jax.random.fold_in(key, 71), 3)
    counts = jax.random.randint(subkeys[0], (N_SPACE, N_TGT, shell_size), 1, SLOT + 1)
    offsets = jnp.arange(shell_size, dtype=jnp.int32) - RANGE
    peer_index = jnp.arange(N_SPACE, dtype=jnp.int32)[:, None, None] + offsets[None, None, :]
    inside = (peer_index >= 0) & (peer_index < N_SPACE)
    counts = jnp.where(inside, counts, 0)
    counts = counts.at[:, :, RANGE].set(SLOT)
    scores = jax.random.randint(subkeys[1], (N_SPACE, N_TGT, shell_size, DROP_DEV), 0, 1 << 20) * DROP_DEV + jnp.arange(DROP_DEV, dtype=jnp.int32)
    drop_order = jnp.argsort(scores, axis=-1)[..., :SLOT].astype(jnp.int32)
    return (counts.astype(jnp.int32), drop_order, subkeys[2])


def draw_send_count(key, part):
    return shell_tables(key)[0]


def draw_send_list(key, part):
    return shell_tables(key)[1]


def draw_pair_slot(key, part):
    shell_size = 2 * RANGE + 1
    counts, drop_order, rest_key = shell_tables(key)
    subkeys = jax.random.split(rest_key, 3)
    group_slot = jax.random.randint(subkeys[0], (N_SPACE, N_TGT, PAIRS), 0, N_TGT)
    offset = jax.random.randint(subkeys[1], (N_SPACE, N_TGT, PAIRS), 0, shell_size)
    space_ids = jnp.arange(N_SPACE, dtype=jnp.int32)[:, None, None]
    sender = space_ids - offset + RANGE
    usable = (sender >= 0) & (sender < N_SPACE)
    offset = jnp.where(usable, offset, RANGE)
    sender = jnp.where(usable, sender, space_ids + jnp.zeros_like(sender))
    live_count = counts[sender, group_slot, offset]
    raw_draw = jax.random.randint(subkeys[2], (N_SPACE, N_TGT, PAIRS), 0, 1 << 20)
    within = raw_draw % live_count
    return ((group_slot * shell_size + offset) * SLOT + within).astype(jnp.int32)


def surface_shapes(key):
    subkeys = jax.random.split(jax.random.fold_in(key, 13), 3)
    raw_draw = jax.random.normal(subkeys[0], (DROPS, 3, NC), jnp.float32)
    length = jnp.sqrt(jnp.sum(raw_draw * raw_draw, axis=1, keepdims=True) + 1e-12)
    unit_vector = raw_draw / length
    center = jax.random.uniform(subkeys[1], (DROPS, 3, 1), jnp.float32, -1.5, 1.5)
    radius = jax.random.uniform(subkeys[2], (DROPS, 1, 1), jnp.float32, 0.7, 1.3)
    return (center + radius * unit_vector, unit_vector)


def draw_positions(key, part):
    return surface_shapes(key)[0]


def draw_normals(key, part):
    return surface_shapes(key)[1]


def touch_ends(result, own_key, least, largest):
    index_at = [jax.random.randint(jax.random.fold_in(own_key, axis), (), 0, length) for axis, length in enumerate(result.shape)]
    longest = result.shape.index(max(result.shape))
    neighbour = index_at[:longest] + [(index_at[longest] + 1) % result.shape[longest]] + index_at[longest + 1:]
    return result.at[tuple(index_at)].set(least).at[tuple(neighbour)].set(largest)


def shard_levels(own_key, dims, cuts, low, high):
    level, own = 1.0, jax.random.fold_in(own_key, 6)
    for dim, shards_of in cuts:
        heights = jnp.exp(jax.random.uniform(jax.random.fold_in(own, dim), (shards_of,), jnp.float32, low / len(cuts), high / len(cuts)))
        level = level * jnp.repeat(heights, dims[dim] // shards_of).reshape([-1 if axis == dim else 1 for axis in range(len(dims))])
    return level


def profile(number_of, total, most, lean):
    loads = [(1 << 20) // math.isqrt(standing ** lean) + 1 for standing in range(2, number_of + 1)]
    spare, given = total - most - (number_of - 1), [1] * (number_of - 1)
    while spare > 0:
        movable = [i for i in range(number_of - 1) if given[i] < most]
        whole, remaining = sum([loads[i] for i in movable]), spare
        for i in movable:
            addition = min(most - given[i], max(1, remaining * loads[i] // whole), spare)
            given[i] = given[i] + addition
            spare = spare - addition
    return np.array([most] + given)


def uneven(stream_key, amount, total, most, skew):
    if amount == 2:
        one = jax.random.randint(stream_key, (), max(1, total - most), min(most, total - 1) + 1)
        return jnp.stack([one, total - one])
    sizes = jnp.asarray(profile(amount, total, most, skew), jnp.int32)
    twos = (amount - 1) // 2
    giver, sink = sizes[1:1 + 2 * twos:2], sizes[2:2 + 2 * twos:2]
    slack = jnp.minimum(giver - 1, most - sink)
    moved = jax.random.randint(jax.random.fold_in(stream_key, 1), (twos,), 0, 1 << 20) % (slack + 1)
    sizes = sizes.at[1:1 + 2 * twos:2].set(giver - moved).at[2:2 + 2 * twos:2].set(sink + moved)
    return sizes[jax.random.permutation(jax.random.fold_in(stream_key, 2), amount)]


def noise(rng, shape, deviation, bound, shards=(), kind=jnp.bfloat16):
    values = deviation * jax.random.normal(rng, shape, jnp.float32)
    if shards:
        values = values * shard_levels(rng, shape, shards, -0.22, 0.18)
    return jnp.clip(values, -bound, bound).astype(kind)


def setup_inputs(seed: int = 0) -> dict:
    arg_keys = jax.random.split(jax.random.key(seed), 12)
    positions = draw_positions(jax.random.fold_in(arg_keys[11], 71), 0)
    normals = draw_normals(jax.random.fold_in(arg_keys[11], 71), 0)
    charge = noise(arg_keys[2], (DROPS, NC), 1.0, 6.0, ((0, 512),), jnp.float32)
    weights = jnp.clip(jnp.exp(math.log(2.0) - 1.3862944 * jax.random.uniform(arg_keys[3], (DROPS, NC), jnp.float32) ** shard_levels(arg_keys[3], (DROPS, NC), ((0, 512),), -0.2, 0.2)), 0.5, 2.0)
    applied = noise(arg_keys[4], (3,), 1.0, 3.0, (), jnp.float32)
    upsample = noise(arg_keys[5], (NC, NU), NC ** -0.5, 0.25)
    send_list = draw_send_list(jax.random.fold_in(arg_keys[11], 71), 0)
    send_count = draw_send_count(jax.random.fold_in(arg_keys[11], 71), 0)
    pair_slot = draw_pair_slot(jax.random.fold_in(arg_keys[11], 71), 0)
    pair_tile = touch_ends(jax.random.randint(arg_keys[9], (N_SPACE, N_TGT, PAIRS), 0, 2 * DROP_DEV), jax.random.fold_in(arg_keys[9], 1), 0, (2 * DROP_DEV) - 1).astype(jnp.int32)
    pair_count = jax.vmap(lambda own: uneven(own, N_TGT, GROUP_PAIRS, PAIRS, 2))(jax.random.split(arg_keys[10], N_SPACE)).reshape((N_SPACE, N_TGT)).astype(jnp.int32)
    return dict(positions=positions, normals=normals, charge=charge, weights=weights, applied=applied, upsample=upsample, send_list=send_list, send_count=send_count, pair_slot=pair_slot, pair_tile=pair_tile, pair_count=pair_count)


reg_square = 0.25

def field_term(source, target):
    apart = target[:, None, :] - source[:3, :, None]
    dist_sq = lax.optimization_barrier(jnp.sum(apart * apart, axis=0)) + reg_square
    inverse = lax.rsqrt(dist_sq)
    strength = source[3][:, None] * inverse * inverse * inverse
    return lax.optimization_barrier(jnp.sum(apart * strength[None], axis=1)) / (4.0 * math.pi)

def stokes_term(source_pos, source_force, target):
    apart = target[:, None, :] - source_pos[:, :, None]
    dist_sq = lax.optimization_barrier(jnp.sum(apart * apart, axis=0)) + reg_square
    inverse = lax.rsqrt(dist_sq)
    cube = inverse * inverse * inverse
    along = lax.optimization_barrier(jnp.sum(apart * source_force[:, :, None], axis=0))
    first = source_force[:, :, None] * ((dist_sq + reg_square) * cube)[None]
    second = apart * (along * cube)[None]
    return lax.optimization_barrier(jnp.sum(first + second, axis=1)) / (8.0 * math.pi)

def to_tiles(array):
    count_d, comps, nodes = array.shape
    return array.reshape(count_d, comps, 2, nodes // 2).transpose(0, 2, 1, 3).reshape(count_d * 2, comps, nodes // 2)

def from_tiles(array):
    count_d = array.shape[0] // 2
    comps = array.shape[1]
    half_nodes = array.shape[2]
    return array.reshape(count_d, 2, comps, half_nodes).transpose(0, 2, 1, 3).reshape(count_d, comps, 2 * half_nodes)

def reference(positions, normals, charge, weights, applied, upsample, send_list, send_count, pair_slot, pair_tile, pair_count):
    shell_size = 2 * RANGE + 1
    drop_count = positions.shape[0]
    payload = jnp.concatenate([positions, (charge * weights)[:, None, :]], axis=1).astype(jnp.bfloat16)
    source_fine = jnp.dot(payload.reshape(drop_count * 4, NC), upsample, preferred_element_type=jnp.float32).reshape(drop_count, 4, NU)
    space_ids = jnp.arange(N_SPACE, dtype=jnp.int32)[:, None, None]
    tgt_ids = jnp.arange(N_TGT, dtype=jnp.int32)[None, :, None]
    group_slot = pair_slot // (shell_size * SLOT)
    offset = pair_slot // SLOT % shell_size
    within = pair_slot % SLOT
    sender = space_ids - offset + RANGE
    inside = (sender >= 0) & (sender < N_SPACE)
    sender = jnp.clip(sender, 0, N_SPACE - 1)
    local_drop = send_list[sender, group_slot, offset, within]
    slot_live = inside & (within < send_count[sender, group_slot, offset])
    pair_live = jnp.arange(PAIRS, dtype=jnp.int32)[None, None, :] < pair_count[:, :, None]
    live_mask = (slot_live & pair_live).astype(jnp.float32).reshape(-1)
    source_drop = ((sender * N_TGT + group_slot) * DROP_DEV + local_drop).astype(jnp.int32)
    tile_index = ((space_ids * N_TGT + tgt_ids) * (2 * DROP_DEV) + pair_tile).astype(jnp.int32)
    target_tiles = to_tiles(positions)
    batch_sources = source_drop.reshape(N_SPACE, N_TGT * PAIRS)
    batch_tiles = tile_index.reshape(N_SPACE, N_TGT * PAIRS)

    def first_one(drop_id, tile_id):
        return field_term(source_fine[drop_id], target_tiles[tile_id])

    def first_batch(items):
        return jax.vmap(first_one)(items[0], items[1])
    field_terms = lax.map(first_batch, (batch_sources, batch_tiles)).reshape(-1, 3, NC // 2)
    flat_tiles = tile_index.reshape(-1)
    near_field = jnp.zeros(target_tiles.shape, jnp.float32).at[flat_tiles].add(field_terms * live_mask[:, None, None])
    field_sum = applied[None, :, None] + near_field
    normal_tiles = to_tiles(normals)
    normal_part = lax.optimization_barrier(jnp.sum(field_sum * normal_tiles, axis=1, keepdims=True))
    traction_tiles = normal_part * field_sum - 0.5 * lax.optimization_barrier(jnp.sum(field_sum * field_sum, axis=1, keepdims=True)) * normal_tiles
    traction = from_tiles(traction_tiles)
    force_payload = (traction * weights[:, None, :]).astype(jnp.bfloat16)
    force_fine = jnp.dot(force_payload.reshape(drop_count * 3, NC), upsample, preferred_element_type=jnp.float32).reshape(drop_count, 3, NU)

    def second_one(drop_id, tile_id):
        return stokes_term(source_fine[drop_id][:3], force_fine[drop_id], target_tiles[tile_id])

    def second_batch(items):
        return jax.vmap(second_one)(items[0], items[1])
    flow_terms = lax.map(second_batch, (batch_sources, batch_tiles)).reshape(-1, 3, NC // 2)
    velocity_tiles = jnp.zeros(target_tiles.shape, jnp.float32).at[flat_tiles].add(flow_terms * live_mask[:, None, None])
    velocity = from_tiles(velocity_tiles)
    return (traction, velocity)
```

```python
import functools
import math

import jax
import jax.numpy as jnp
from jax import lax
from jax.experimental import pallas as pl
from jax.experimental.pallas import tpu as pltpu
from jax.sharding import Mesh
from jax.sharding import PartitionSpec as P

REG = 0.25
VMEM = pl.BlockSpec(memory_space=pltpu.VMEM)
SMEM = pl.BlockSpec(memory_space=pltpu.SMEM)


def ceil_to(n, m):
    return -(-n // m) * m


def iota(shape, dim):
    return lax.broadcasted_iota(jnp.int32, shape, dim)


def split3(x):
    high = x.astype(jnp.bfloat16).astype(jnp.float32)
    rest = x - high
    mid = rest.astype(jnp.bfloat16).astype(jnp.float32)
    low = (rest - mid).astype(jnp.bfloat16).astype(jnp.float32)
    return high, mid, low


def pack_kernel(nodes, send_ref, pos_ref, charge_ref, weight_ref, out_ref, block):
    drops = pos_ref.shape[0]
    lanes = block.shape[1]
    block[...] = jnp.zeros_like(block)
    for d in range(drops):
        block[d * 4 : d * 4 + 3, 0:nodes] = pos_ref[d]
        block[d * 4 + 3 : d * 4 + 4, 0:nodes] = (
            charge_ref[d : d + 1, :] * weight_ref[d : d + 1, :]
        )
    base = nodes - (lanes - 128)
    lane = iota((1, 128), 1)
    row = block[0:1, lanes - 128 : lanes]
    shell, slots = send_ref.shape
    for o in range(shell):
        for j in range(slots):
            row = jnp.where(
                lane == base + o * slots + j, send_ref[o, j].astype(jnp.float32), row
            )
    block[0:1, lanes - 128 : lanes] = row
    packed = block[...].astype(jnp.bfloat16)
    for i in range(out_ref.shape[0]):
        out_ref[i] = packed


def fetch_blocks(slot_ref, below_ref, own_ref, above_ref, rows):
    core = lax.axis_index("core")
    pairs = slot_ref.shape[0]
    for k in range(pairs):
        p = slot_ref[k]
        owner = p // 20
        place = core + 4 - (p // 4) % 5
        chip = place // 2
        index = (place % 2) * 4 + owner
        for which, ref in enumerate((below_ref, own_ref, above_ref)):

            @pl.when(chip == which)
            def _(ref=ref, k=k, index=index):
                rows[k * 16 : (k + 1) * 16, :] = ref[index]


def tile_slices(nodes):
    half = nodes // 2
    return [(0, half), (half, nodes)]


def centred(pos, half, height):
    mean = jnp.sum(pos, axis=1, keepdims=True) / half
    return pos - mean, mean


def field_kernel(
    nodes,
    slot_ref,
    tile_ref,
    count_ref,
    applied_ref,
    below_ref,
    own_ref,
    above_ref,
    up_ref,
    pos_ref,
    normal_ref,
    weight_ref,
    trac_ref,
    send_ref,
    cube_ref,
    hot_ref,
    fine_ref,
    rows,
    block,
    targets,
    means,
    feats,
    near,
):
    pairs = slot_ref.shape[0]
    drops = pos_ref.shape[0]
    half = nodes // 2
    wide = feats.shape[1]
    lanes = rows.shape[1]
    fine_nodes = up_ref.shape[1]

    fetch_blocks(slot_ref, below_ref, own_ref, above_ref, rows)
    height = pairs * 8
    base = nodes - (lanes - 128)
    row_id = iota((height, 128), 0)
    lane_id = iota((height, 128), 1)
    want = jnp.zeros((height, 128), jnp.int32)
    table = []
    for k in range(pairs):
        want = jnp.where(row_id // 8 == k, base + slot_ref[k] % 20, want)
        head = rows[k * 16 : (k + 1) * 16, lanes - 128 : lanes].astype(jnp.float32)[0:1]
        table.append(jnp.broadcast_to(head, (8, 128)))
    table = jnp.concatenate(table, axis=0)
    chosen = jnp.sum(jnp.where(lane_id == want, table, 0.0), axis=1, keepdims=True)
    column = (row_id // 8) * 16 + row_id % 4 + 4 * chosen.astype(jnp.int32)
    hot = (lane_id == column).astype(jnp.float32).astype(jnp.bfloat16)
    hot_ref[...] = hot
    picked = jnp.dot(hot, rows[...], preferred_element_type=jnp.float32)
    fine = jnp.dot(
        picked[:, 0:nodes].astype(jnp.bfloat16),
        up_ref[...],
        preferred_element_type=jnp.float32,
    )
    for k in range(pairs):
        fine_ref[k] = fine[k * 8 : (k + 1) * 8]

    near[...] = jnp.zeros_like(near)
    targets[...] = jnp.zeros_like(targets)
    for d in range(drops):
        for h, (lo, hi) in enumerate(tile_slices(nodes)):
            b = d * 2 + h
            pos, mean = centred(pos_ref[d, :, lo:hi], half, 8)
            targets[b, 0:3, 0:half] = pos
            means[b, 0:3, :] = jnp.broadcast_to(mean, (3, 128))
            means[b, 3:8, :] = jnp.zeros((5, 128), jnp.float32)
    sub = iota((8, wide), 0)
    for b in range(2 * drops):
        t = targets[b]
        norm = jnp.sum(t * t, axis=0, keepdims=True)
        t8 = jnp.where(sub < 4, t, jnp.concatenate([t[4:8], t[0:4]], axis=0))
        t8 = jnp.where(sub % 4 == 3, 1.0, t8)
        high, mid, low = split3(t8)
        nh, nm, nl = split3(norm)
        last = jnp.where(
            sub == 0, nh, jnp.where(sub == 1, nm, jnp.where(sub == 2, nl, 0.0))
        )
        stack = jnp.concatenate([high, mid, jnp.where(sub < 4, high, low), last], axis=0)
        feats[b] = stack.T.astype(jnp.bfloat16)

    sub_f = iota((8, fine_nodes), 0)

    def pair(k, carry):
        b = tile_ref[k]
        f = fine_ref[k]
        m = means[b, :, 0:1]
        m8 = jnp.where(iota((8, 1), 0) < 4, m, jnp.concatenate([m[4:8], m[0:4]], axis=0))
        charge = f[3:4]
        y = f - m8
        y_only = jnp.where(sub_f < 3, y, 0.0)
        norm = jnp.sum(y_only * y_only, axis=0, keepdims=True) + REG
        q = jnp.where(sub_f % 4 == 3, norm, -2.0 * y)
        high, mid, low = split3(q)
        first = jnp.where(sub_f < 4, high, mid)
        second = jnp.where(sub_f < 4, low, high)
        third = jnp.where(sub_f < 3, 1.0, 0.0)
        src = jnp.concatenate([first, first, second, third], axis=0).astype(jnp.bfloat16)
        coef = jnp.where(sub_f % 4 == 3, charge, charge * y)
        high, mid, low = split3(coef)
        coefs = jnp.concatenate(
            [jnp.where(sub_f < 4, high, mid), jnp.where(sub_f < 4, low, 0.0)], axis=0
        ).astype(jnp.bfloat16)
        tgt = feats[b]
        total = jnp.zeros((wide, 16), jnp.float32)
        for lo in range(0, fine_nodes, 256):
            hi = min(lo + 256, fine_nodes)
            dist = jnp.dot(tgt, src[:, lo:hi], preferred_element_type=jnp.float32)
            inv = lax.rsqrt(jnp.maximum(dist, REG))
            cube = (inv * inv * inv).astype(jnp.bfloat16)
            cube_ref[k, :, lo:hi] = cube
            total = total + lax.dot_general(
                cube,
                coefs[:, lo:hi],
                (((1,), (1,)), ((), ())),
                preferred_element_type=jnp.float32,
            )
        sums = total.T
        sums = sums[0:8] + sums[8:16]
        sums = sums + jnp.concatenate([sums[4:8], sums[0:4]], axis=0)
        near[b] += (targets[b] * sums[3:4] - sums) * (1.0 / (4.0 * math.pi))
        return carry

    lax.fori_loop(0, count_ref[0], pair, 0)

    block[...] = jnp.zeros_like(block)
    for d in range(drops):
        for h, (lo, hi) in enumerate(tile_slices(nodes)):
            e = near[d * 2 + h][0:3, 0:half]
            part = []
            for c in range(3):
                part.append(e[c : c + 1] + applied_ref[c])
            e = jnp.concatenate(part, axis=0)
            n = normal_ref[d, :, lo:hi]
            along = jnp.sum(e * n, axis=0, keepdims=True)
            square = jnp.sum(e * e, axis=0, keepdims=True)
            t = along * e - 0.5 * square * n
            trac_ref[d, :, lo:hi] = t
            block[d * 4 : d * 4 + 3, lo:hi] = t * weight_ref[d : d + 1, lo:hi]
    packed = block[...].astype(jnp.bfloat16)
    for i in range(send_ref.shape[0]):
        send_ref[i] = packed


def stokes_kernel(
    nodes,
    slot_ref,
    tile_ref,
    count_ref,
    below_ref,
    own_ref,
    above_ref,
    up_ref,
    pos_ref,
    cube_ref,
    hot_ref,
    fine_ref,
    vel_ref,
    rows,
    targets,
    means,
    forces,
    flow,
):
    pairs = slot_ref.shape[0]
    drops = pos_ref.shape[0]
    half = nodes // 2
    fine_nodes = up_ref.shape[1]
    wide = targets.shape[2]

    fetch_blocks(slot_ref, below_ref, own_ref, above_ref, rows)
    picked = jnp.dot(hot_ref[...], rows[...], preferred_element_type=jnp.float32)
    fine = jnp.dot(
        picked[:, 0:nodes].astype(jnp.bfloat16),
        up_ref[...],
        preferred_element_type=jnp.float32,
    )
    for k in range(pairs):
        forces[k] = fine[k * 8 : (k + 1) * 8]

    flow[...] = jnp.zeros_like(flow)
    targets[...] = jnp.zeros_like(targets)
    for d in range(drops):
        for h, (lo, hi) in enumerate(tile_slices(nodes)):
            b = d * 2 + h
            pos, mean = centred(pos_ref[d, :, lo:hi], half, 8)
            targets[b, 0:3, 0:half] = pos
            means[b, 0:3, :] = jnp.broadcast_to(mean, (3, 128))
            means[b, 3:8, :] = jnp.zeros((5, 128), jnp.float32)

    sub_f = iota((8, fine_nodes), 0)

    def pair(k, carry):
        b = tile_ref[k]
        m = means[b, :, 0:1]
        m8 = jnp.where(iota((8, 1), 0) < 4, m, jnp.concatenate([m[4:8], m[0:4]], axis=0))
        y = fine_ref[k] - m8
        f = forces[k]
        y_only = jnp.where(sub_f < 3, y, 0.0)
        norm = jnp.sum(y_only * y_only, axis=0, keepdims=True)
        dot = jnp.sum(y_only * f, axis=0, keepdims=True)
        one = f * jnp.where(sub_f < 4, 1.0, norm)
        two = f * jnp.where(sub_f < 4, y[0:1], y[1:2])
        three = jnp.where(sub_f < 4, f * y[2:3], dot * y)
        parts = [split3(one), split3(two), split3(three)]
        coefs = jnp.concatenate(
            [parts[g][s] for s in range(3) for g in range(3)]
            + [jnp.zeros((8, fine_nodes), jnp.float32)],
            axis=0,
        ).astype(jnp.bfloat16)
        total = jnp.zeros((wide, 80), jnp.float32)
        for lo in range(0, fine_nodes, 256):
            hi = min(lo + 256, fine_nodes)
            total = total + lax.dot_general(
                cube_ref[k, :, lo:hi],
                coefs[:, lo:hi],
                (((1,), (1,)), ((), ())),
                preferred_element_type=jnp.float32,
            )
        sums = total.T
        sums = sums[0:24] + sums[24:48] + sums[48:72]
        x = targets[b][0:3]
        force, force_sq = sums[0:3], sums[4:7]
        t0, t1, t2 = sums[8:11], sums[12:15], sums[16:19]
        last = sums[20:23]
        x0, x1, x2 = x[0:1], x[1:2], x[2:3]
        square = x0 * x0 + x1 * x1 + x2 * x2
        trace = t0[0:1] + t1[1:2] + t2[2:3]
        reach = jnp.sum(x * force, axis=0, keepdims=True) - trace
        mixed = jnp.concatenate(
            [jnp.sum(x * t, axis=0, keepdims=True) for t in (t0, t1, t2)], axis=0
        )
        v = (square + 2.0 * REG) * force + force_sq
        v = v - 2.0 * (x0 * t0 + x1 * t1 + x2 * t2) + x * reach - mixed + last
        flow[b, 0:3, :] += v * (1.0 / (8.0 * math.pi))
        return carry

    lax.fori_loop(0, count_ref[0], pair, 0)
    for d in range(drops):
        for h, (lo, hi) in enumerate(tile_slices(nodes)):
            vel_ref[d, :, lo:hi] = flow[d * 2 + h][0:3, 0:half]


def exchange(mine, chips):
    own = lax.all_to_all(mine, ("core", "tgt"), 0, 0)
    below = lax.ppermute(own, "chip", [(i, i + 1) for i in range(chips - 1)])
    above = lax.ppermute(own, "chip", [(i + 1, i) for i in range(chips - 1)])
    return below, own, above


def local(
    chips,
    positions,
    normals,
    charge,
    weights,
    applied,
    upsample,
    send_list,
    send_count,
    pair_slot,
    pair_tile,
    pair_count,
):
    drops, _, nodes = positions.shape
    fine_nodes = upsample.shape[1]
    pairs = pair_slot.shape[2]
    lanes = ceil_to(nodes + 20, 128)
    wide = ceil_to(nodes // 2, 16)
    tiles = 2 * drops
    f32, bf16 = jnp.float32, jnp.bfloat16
    slots, tile_ids, count = pair_slot[0, 0], pair_tile[0, 0], pair_count[0]

    mine = pl.pallas_call(
        functools.partial(pack_kernel, nodes),
        out_shape=jax.ShapeDtypeStruct((8, 16, lanes), bf16),
        in_specs=[SMEM, VMEM, VMEM, VMEM],
        out_specs=VMEM,
        scratch_shapes=[pltpu.VMEM((16, lanes), f32)],
        name="pack",
    )(send_list[0, 0], positions, charge, weights)
    gathered = exchange(mine, chips)

    traction, forces, cubes, hot, fine = pl.pallas_call(
        functools.partial(field_kernel, nodes),
        out_shape=(
            jax.ShapeDtypeStruct((drops, 3, nodes), f32),
            jax.ShapeDtypeStruct((8, 16, lanes), bf16),
            jax.ShapeDtypeStruct((pairs, wide, fine_nodes), bf16),
            jax.ShapeDtypeStruct((pairs * 8, 128), bf16),
            jax.ShapeDtypeStruct((pairs, 8, fine_nodes), f32),
        ),
        in_specs=[SMEM] * 4 + [VMEM] * 7,
        out_specs=(VMEM,) * 5,
        scratch_shapes=[
            pltpu.VMEM((pairs * 16, lanes), bf16),
            pltpu.VMEM((16, lanes), f32),
            pltpu.VMEM((tiles, 8, wide), f32),
            pltpu.VMEM((tiles, 8, 128), f32),
            pltpu.VMEM((tiles, wide, 32), bf16),
            pltpu.VMEM((tiles, 8, wide), f32),
        ],
        name="field",
    )(slots, tile_ids, count, applied, *gathered, upsample, positions, normals, weights)
    gathered = exchange(forces, chips)

    velocity = pl.pallas_call(
        functools.partial(stokes_kernel, nodes),
        out_shape=jax.ShapeDtypeStruct((drops, 3, nodes), f32),
        in_specs=[SMEM] * 3 + [VMEM] * 8,
        out_specs=VMEM,
        scratch_shapes=[
            pltpu.VMEM((pairs * 16, lanes), bf16),
            pltpu.VMEM((tiles, 8, wide), f32),
            pltpu.VMEM((tiles, 8, 128), f32),
            pltpu.VMEM((pairs, 8, fine_nodes), f32),
            pltpu.VMEM((tiles, 8, wide), f32),
        ],
        name="stokes",
    )(slots, tile_ids, count, *gathered, upsample, positions, cubes, hot, fine)
    return traction, velocity


def solution(mesh):
    space, tgt = mesh.shape["space"], mesh.shape["tgt"]
    chips = space // 2
    fine_mesh = Mesh(mesh.devices.reshape(chips, 2, tgt), ("chip", "core", "tgt"))
    every = ("chip", "core", "tgt")
    rows = ("chip", "core")
    placed = (
        P(every, None, None),
        P(every, None, None),
        P(every, None),
        P(every, None),
        P(),
        P(),
        P(rows, "tgt", None, None),
        P(rows, "tgt", None),
        P(rows, "tgt", None),
        P(rows, "tgt", None),
        P(rows, "tgt"),
    )
    return jax.shard_map(
        functools.partial(local, chips),
        mesh=fine_mesh,
        in_specs=placed,
        out_specs=(P(every, None, None), P(every, None, None)),
        check_vma=False,
    )
```

```python
import functools
import math

import jax
import jax.numpy as jnp
from jax import lax
from jax.experimental import pallas as pl
from jax.experimental.pallas import tpu as pltpu
from jax.sharding import Mesh
from jax.sharding import PartitionSpec as P

REG = 0.25
VMEM = pl.BlockSpec(memory_space=pltpu.VMEM)
HBM = pl.BlockSpec(memory_space=pltpu.HBM)
SMEM = pl.BlockSpec(memory_space=pltpu.SMEM)
LIMIT = (2 << 20, 20 << 20, 20 << 20)


def ceil_to(n, m):
    return -(-n // m) * m


def iota(shape, dim):
    return lax.broadcasted_iota(jnp.int32, shape, dim)


def split3(x):
    high = x.astype(jnp.bfloat16).astype(jnp.float32)
    rest = x - high
    mid = rest.astype(jnp.bfloat16).astype(jnp.float32)
    low = (rest - mid).astype(jnp.bfloat16).astype(jnp.float32)
    return high, mid, low


def fetch_all(pairs, sems):
    copies = [
        pltpu.make_async_copy(src, dst, sems.at[i]) for i, (src, dst) in enumerate(pairs)
    ]
    for copy in copies:
        copy.start()
    return copies


def pack_kernel(
    nodes, send_hbm, pos_hbm, charge_hbm, weight_hbm, out_ref,
    send_ref, pos_ref, charge_ref, weight_ref, block, sems,
):
    copies = fetch_all(
        [
            (send_hbm, send_ref),
            (pos_hbm, pos_ref),
            (charge_hbm, charge_ref),
            (weight_hbm, weight_ref),
        ],
        sems,
    )
    lanes = block.shape[1]
    block[...] = jnp.zeros_like(block)
    for copy in copies:
        copy.wait()
    for c in range(3):
        block[c * 4 : (c + 1) * 4, 0:nodes] = pos_ref[c]
    block[12:16, 0:nodes] = charge_ref[...] * weight_ref[...]
    base = nodes - (lanes - 128)
    lane = iota((1, 128), 1)
    row = block[0:1, lanes - 128 : lanes]
    slots, shell = send_ref.shape
    for o in range(shell):
        for j in range(slots):
            row = jnp.where(
                lane == base + o * slots + j, send_ref[j, o].astype(jnp.float32), row
            )
    block[0:1, lanes - 128 : lanes] = row
    packed = block[...].astype(jnp.bfloat16)
    for i in range(out_ref.shape[0]):
        out_ref[i] = packed


def fetch_blocks(slot_ref, own_ref, side_ref, rows):
    core = lax.axis_index("core")
    for k in range(slot_ref.shape[1]):
        p = slot_ref[0, k]
        owner = p // 20
        place = core + 4 - (p // 4) % 5
        chip = place // 2
        index = (place % 2) * 4 + owner
        for which, ref in enumerate((side_ref.at[0], own_ref, side_ref.at[1])):

            @pl.when(chip == which)
            def _(ref=ref, k=k, index=index):
                rows[k * 16 : (k + 1) * 16, :] = ref[index]


def tile_slices(nodes):
    half = nodes // 2
    return [(0, half), (half, nodes)]


def target_kernel(pos_hbm, up_hbm, feat_ref, target_ref, mean_ref, up_ref, pos_ref, sems):
    copies = fetch_all([(pos_hbm, pos_ref), (up_hbm, up_ref)], sems)
    copies[0].wait()
    drops, nodes = pos_ref.shape[1:]
    half = nodes // 2
    wide = feat_ref.shape[1]
    target_ref[...] = jnp.zeros_like(target_ref)
    mean_ref[...] = jnp.zeros_like(mean_ref)
    for d in range(drops):
        for h, (lo, hi) in enumerate(tile_slices(nodes)):
            for c in range(3):
                row = pos_ref[c, d : d + 1, lo:hi]
                mean = jnp.sum(row, axis=1, keepdims=True) / half
                target_ref[d * 2 + h, c : c + 1, 0:half] = row - mean
                mean_ref[d * 2 + h, c : c + 1, :] = jnp.broadcast_to(mean, (1, 128))
                mean_ref[d * 2 + h, c + 4 : c + 5, :] = jnp.broadcast_to(mean, (1, 128))
    sub = iota((8, wide), 0)
    for b in range(2 * drops):
        t = target_ref[b]
        norm = jnp.sum(t * t, axis=0, keepdims=True)
        t8 = jnp.where(sub < 4, t, jnp.concatenate([t[4:8], t[0:4]], axis=0))
        t8 = jnp.where(sub % 4 == 3, 1.0, t8)
        high, mid, low = split3(t8)
        nh, nm, nl = split3(norm)
        last = jnp.where(
            sub == 0, nh, jnp.where(sub == 1, nm, jnp.where(sub == 2, nl, 0.0))
        )
        stack = jnp.concatenate([high, mid, jnp.where(sub < 4, high, low), last], axis=0)
        feat_ref[b] = stack.T.astype(jnp.bfloat16)
    copies[1].wait()


def field_kernel(
    nodes,
    count_ref,
    slot_hbm,
    tile_hbm,
    applied_hbm,
    normal_hbm,
    weight_hbm,
    own_ref,
    side_ref,
    up_ref,
    feats,
    targets,
    means,
    trac_ref,
    send_ref,
    cube_ref,
    hot_ref,
    fine_ref,
    slot_ref,
    tile_ref,
    applied_ref,
    normal_ref,
    weight_ref,
    rows,
    block,
    near,
    field,
    src_a,
    src_b,
    coef_a,
    coef_b,
    sems,
):
    copies = fetch_all(
        [
            (slot_hbm, slot_ref),
            (tile_hbm, tile_ref),
            (applied_hbm, applied_ref),
            (normal_hbm, normal_ref),
            (weight_hbm, weight_ref),
        ],
        sems,
    )
    pairs = slot_ref.shape[1]
    drops = weight_ref.shape[0]
    half = nodes // 2
    wide = feats.shape[1]
    lanes = rows.shape[1]
    fine_nodes = up_ref.shape[1]
    near[...] = jnp.zeros_like(near)
    block[...] = jnp.zeros_like(block)
    for copy in copies[:3]:
        copy.wait()

    fetch_blocks(slot_ref, own_ref, side_ref, rows)
    height = pairs * 8
    base = nodes - (lanes - 128)
    row_id = iota((height, 128), 0)
    lane_id = iota((height, 128), 1)
    want = jnp.zeros((height, 128), jnp.int32)
    table = []
    for k in range(pairs):
        want = jnp.where(row_id // 8 == k, base + slot_ref[0, k] % 20, want)
        head = rows[k * 16 : (k + 1) * 16, lanes - 128 : lanes].astype(jnp.float32)[0:1]
        table.append(jnp.broadcast_to(head, (8, 128)))
    table = jnp.concatenate(table, axis=0)
    chosen = jnp.sum(jnp.where(lane_id == want, table, 0.0), axis=1, keepdims=True)
    column = (row_id // 8) * 16 + (row_id % 4) * 4 + chosen.astype(jnp.int32)
    hot = (lane_id == column).astype(jnp.float32).astype(jnp.bfloat16)
    hot_ref[...] = hot
    picked = jnp.dot(hot, rows[...], preferred_element_type=jnp.float32)
    fine = jnp.dot(
        picked[:, 0:nodes].astype(jnp.bfloat16),
        up_ref[...],
        preferred_element_type=jnp.float32,
    )
    for k in range(pairs):
        fine_ref[k] = fine[k * 8 : (k + 1) * 8]

    sub_f = iota((8, fine_nodes), 0)

    def prepare(k, src, coefs):
        f = fine_ref[k]
        charge = f[3:4]
        y = f - means[tile_ref[0, k], :, 0:1]
        y_only = jnp.where(sub_f < 3, y, 0.0)
        norm = jnp.sum(y_only * y_only, axis=0, keepdims=True) + REG
        q = jnp.where(sub_f % 4 == 3, norm, -2.0 * y)
        high, mid, low = split3(q)
        first = jnp.where(sub_f < 4, high, mid)
        second = jnp.where(sub_f < 4, low, high)
        third = jnp.where(sub_f < 3, 1.0, 0.0)
        src[...] = jnp.concatenate([first, first, second, third], axis=0).astype(jnp.bfloat16)
        coef = jnp.where(sub_f % 4 == 3, charge, charge * y)
        high, mid, low = split3(coef)
        coefs[...] = jnp.concatenate(
            [jnp.where(sub_f < 4, high, mid), jnp.where(sub_f < 4, low, 0.0)], axis=0
        ).astype(jnp.bfloat16)

    def work(k, src, coefs):
        b = tile_ref[0, k]
        tgt = feats[b]
        total = jnp.zeros((wide, 16), jnp.float32)
        for lo in range(0, fine_nodes, 256):
            hi = min(lo + 256, fine_nodes)
            dist = jnp.dot(tgt, src[:, lo:hi], preferred_element_type=jnp.float32)
            inv = lax.rsqrt(jnp.maximum(dist, REG))
            cube = (inv * inv * inv).astype(jnp.bfloat16)
            cube_ref[k, :, lo:hi] = cube
            total = total + lax.dot_general(
                cube,
                coefs[:, lo:hi],
                (((1,), (1,)), ((), ())),
                preferred_element_type=jnp.float32,
            )
        sums = total.T
        sums = sums[0:8] + sums[8:16]
        sums = sums + jnp.concatenate([sums[4:8], sums[0:4]], axis=0)
        value = (targets[b] * sums[3:4] - sums) * (1.0 / (4.0 * math.pi))
        near[b] += jnp.where(k < count_ref[0, 0], value, 0.0)

    prepare(0, src_a, coef_a)

    def two(i, carry):
        k = 2 * i
        prepare(k + 1, src_b, coef_b)
        work(k, src_a, coef_a)
        prepare(jnp.minimum(k + 2, pairs - 1), src_a, coef_a)
        work(k + 1, src_b, coef_b)
        return carry

    lax.fori_loop(0, pairs // 2, two, 0)

    for copy in copies[3:]:
        copy.wait()
    for d in range(drops):
        for h, (lo, hi) in enumerate(tile_slices(nodes)):
            for c in range(3):
                field[c, d : d + 1, lo:hi] = near[d * 2 + h][c : c + 1, 0:half]
    e = [field[c] + applied_ref[0, c] for c in range(3)]
    n = [normal_ref[c] for c in range(3)]
    along = e[0] * n[0] + e[1] * n[1] + e[2] * n[2]
    square = 0.5 * (e[0] * e[0] + e[1] * e[1] + e[2] * e[2])
    for c in range(3):
        t = along * e[c] - square * n[c]
        trac_ref[c] = t
        block[c * 4 : (c + 1) * 4, 0:nodes] = t * weight_ref[...]
    packed = block[...].astype(jnp.bfloat16)
    for i in range(send_ref.shape[0]):
        send_ref[i] = packed


def stokes_kernel(
    nodes,
    count_ref,
    slot_hbm,
    tile_hbm,
    own_ref,
    side_ref,
    up_ref,
    targets,
    means,
    cube_ref,
    hot_ref,
    fine_ref,
    vel_ref,
    slot_ref,
    tile_ref,
    rows,
    forces,
    flow,
    coef_a,
    coef_b,
    sems,
):
    copies = fetch_all(
        [(slot_hbm, slot_ref), (tile_hbm, tile_ref)], sems
    )
    pairs = slot_ref.shape[1]
    drops = vel_ref.shape[1]
    half = nodes // 2
    fine_nodes = up_ref.shape[1]
    wide = targets.shape[2]
    flow[...] = jnp.zeros_like(flow)
    for copy in copies:
        copy.wait()

    fetch_blocks(slot_ref, own_ref, side_ref, rows)
    picked = jnp.dot(hot_ref[...], rows[...], preferred_element_type=jnp.float32)
    fine = jnp.dot(
        picked[:, 0:nodes].astype(jnp.bfloat16),
        up_ref[...],
        preferred_element_type=jnp.float32,
    )
    for k in range(pairs):
        forces[k] = fine[k * 8 : (k + 1) * 8]

    sub_f = iota((8, fine_nodes), 0)

    def prepare(k, coefs):
        y = fine_ref[k] - means[tile_ref[0, k], :, 0:1]
        f = forces[k]
        y_only = jnp.where(sub_f < 3, y, 0.0)
        norm = jnp.sum(y_only * y_only, axis=0, keepdims=True)
        dot = jnp.sum(y_only * f, axis=0, keepdims=True)
        one = f * jnp.where(sub_f < 4, 1.0, norm)
        two = f * jnp.where(sub_f < 4, y[0:1], y[1:2])
        three = jnp.where(sub_f < 4, f * y[2:3], dot * y)
        parts = [split3(one), split3(two), split3(three)]
        coefs[...] = jnp.concatenate(
            [parts[g][s] for s in range(3) for g in range(3)]
            + [jnp.zeros((8, fine_nodes), jnp.float32)],
            axis=0,
        ).astype(jnp.bfloat16)

    def work(k, coefs):
        b = tile_ref[0, k]
        total = jnp.zeros((wide, 80), jnp.float32)
        for lo in range(0, fine_nodes, 256):
            hi = min(lo + 256, fine_nodes)
            total = total + lax.dot_general(
                cube_ref[k, :, lo:hi],
                coefs[:, lo:hi],
                (((1,), (1,)), ((), ())),
                preferred_element_type=jnp.float32,
            )
        sums = total.T
        sums = sums[0:24] + sums[24:48] + sums[48:72]
        x = targets[b][0:3]
        force, force_sq = sums[0:3], sums[4:7]
        t0, t1, t2 = sums[8:11], sums[12:15], sums[16:19]
        last = sums[20:23]
        x0, x1, x2 = x[0:1], x[1:2], x[2:3]
        square = x0 * x0 + x1 * x1 + x2 * x2
        trace = t0[0:1] + t1[1:2] + t2[2:3]
        reach = jnp.sum(x * force, axis=0, keepdims=True) - trace
        mixed = jnp.concatenate(
            [jnp.sum(x * t, axis=0, keepdims=True) for t in (t0, t1, t2)], axis=0
        )
        v = (square + 2.0 * REG) * force + force_sq
        v = v - 2.0 * (x0 * t0 + x1 * t1 + x2 * t2) + x * reach - mixed + last
        v = v * (1.0 / (8.0 * math.pi))
        flow[b, 0:3, :] += jnp.where(k < count_ref[0, 0], v, 0.0)

    prepare(0, coef_a)

    def two_pairs(i, carry):
        k = 2 * i
        prepare(k + 1, coef_b)
        work(k, coef_a)
        prepare(jnp.minimum(k + 2, pairs - 1), coef_a)
        work(k + 1, coef_b)
        return carry

    lax.fori_loop(0, pairs // 2, two_pairs, 0)
    for d in range(drops):
        for h, (lo, hi) in enumerate(tile_slices(nodes)):
            for c in range(3):
                vel_ref[c, d : d + 1, lo:hi] = flow[d * 2 + h][c : c + 1, 0:half]


def exchange(mine, chips):
    own = lax.all_to_all(mine, ("core", "tgt"), 0, 0)
    moves = [(2 * i, 2 * i + 2) for i in range(chips - 1)]
    moves += [(2 * i + 3, 2 * i + 1) for i in range(chips - 1)]
    side = lax.ppermute(own, ("chip", "core"), moves)
    return own, side


def in_hbm(*arrays):
    return [pltpu.with_memory_space_constraint(a, pltpu.HBM) for a in arrays]


def share(side):
    return lax.all_gather(side, "core")


def local(
    chips,
    positions,
    normals,
    charge,
    weights,
    applied,
    upsample,
    send_list,
    send_count,
    pair_slot,
    pair_tile,
    pair_count,
):
    drops, _, nodes = positions.shape
    fine_nodes = upsample.shape[1]
    pairs = pair_slot.shape[2]
    lanes = ceil_to(nodes + 20, 128)
    wide = ceil_to(nodes // 2, 16)
    tiles = 2 * drops
    f32, bf16 = jnp.float32, jnp.bfloat16
    slots, tile_ids, count = pair_slot[0], pair_tile[0], pair_count

    positions = positions.transpose(1, 0, 2)
    normals = normals.transpose(1, 0, 2)

    i32 = jnp.int32
    dma = pltpu.SemaphoreType.DMA
    mine = pl.pallas_call(
        functools.partial(pack_kernel, nodes),
        out_shape=jax.ShapeDtypeStruct((8, 16, lanes), bf16),
        in_specs=[HBM] * 4,
        out_specs=VMEM,
        scratch_shapes=[
            pltpu.SMEM(send_list.shape[:1:-1], i32),
            pltpu.VMEM((3, drops, nodes), f32),
            pltpu.VMEM((drops, nodes), f32),
            pltpu.VMEM((drops, nodes), f32),
            pltpu.VMEM((16, lanes), f32),
            dma((4,)),
        ],
        compiler_params=pltpu.CompilerParams(vmem_limit_bytes=LIMIT[0]),
        name="pack",
    )(*in_hbm(send_list[0, 0].T, positions, charge, weights))
    own, side = exchange(mine, chips)

    feats, targets, means, up = pl.pallas_call(
        target_kernel,
        out_shape=(
            jax.ShapeDtypeStruct((tiles, wide, 32), bf16),
            jax.ShapeDtypeStruct((tiles, 8, wide), f32),
            jax.ShapeDtypeStruct((tiles, 8, 128), f32),
            jax.ShapeDtypeStruct(upsample.shape, bf16),
        ),
        in_specs=[HBM] * 2,
        out_specs=(VMEM,) * 4,
        scratch_shapes=[pltpu.VMEM((3, drops, nodes), f32), dma((2,))],
        compiler_params=pltpu.CompilerParams(vmem_limit_bytes=LIMIT[0]),
        cost_estimate=pl.CostEstimate(
            flops=4_000_000, bytes_accessed=6_000_000, transcendentals=0
        ),
        name="target",
    )(*in_hbm(positions, upsample))

    traction, forces, cubes, hot, fine = pl.pallas_call(
        functools.partial(field_kernel, nodes),
        out_shape=(
            jax.ShapeDtypeStruct((3, drops, nodes), f32),
            jax.ShapeDtypeStruct((8, 16, lanes), bf16),
            jax.ShapeDtypeStruct((pairs, wide, fine_nodes), bf16),
            jax.ShapeDtypeStruct((pairs * 8, 128), bf16),
            jax.ShapeDtypeStruct((pairs, 8, fine_nodes), f32),
        ),
        in_specs=[SMEM] + [HBM] * 5 + [VMEM] * 6,
        out_specs=(VMEM,) * 5,
        scratch_shapes=[
            pltpu.SMEM((1, pairs), i32),
            pltpu.SMEM((1, pairs), i32),
            pltpu.SMEM((1, 3), f32),
            pltpu.VMEM((3, drops, nodes), f32),
            pltpu.VMEM((drops, nodes), f32),
            pltpu.VMEM((pairs * 16, lanes), bf16),
            pltpu.VMEM((16, lanes), f32),
            pltpu.VMEM((tiles, 8, wide), f32),
            pltpu.VMEM((3, drops, nodes), f32),
            pltpu.VMEM((32, fine_nodes), bf16),
            pltpu.VMEM((32, fine_nodes), bf16),
            pltpu.VMEM((16, fine_nodes), bf16),
            pltpu.VMEM((16, fine_nodes), bf16),
            dma((5,)),
        ],
        compiler_params=pltpu.CompilerParams(vmem_limit_bytes=LIMIT[1]),
        name="field",
    )(
        count, *in_hbm(slots, tile_ids, applied[None], normals, weights),
        own, share(side), up, feats, targets, means,
    )
    own, side = exchange(forces, chips)

    velocity = pl.pallas_call(
        functools.partial(stokes_kernel, nodes),
        out_shape=jax.ShapeDtypeStruct((3, drops, nodes), f32),
        in_specs=[SMEM] + [HBM] * 2 + [VMEM] * 8,
        out_specs=VMEM,
        scratch_shapes=[
            pltpu.SMEM((1, pairs), i32),
            pltpu.SMEM((1, pairs), i32),
            pltpu.VMEM((pairs * 16, lanes), bf16),
            pltpu.VMEM((pairs, 8, fine_nodes), f32),
            pltpu.VMEM((tiles, 8, wide), f32),
            pltpu.VMEM((80, fine_nodes), bf16),
            pltpu.VMEM((80, fine_nodes), bf16),
            dma((2,)),
        ],
        compiler_params=pltpu.CompilerParams(vmem_limit_bytes=LIMIT[2]),
        name="stokes",
    )(count, *in_hbm(slots, tile_ids), own, share(side), up, targets, means, cubes, hot, fine)
    return traction.transpose(1, 0, 2), velocity.transpose(1, 0, 2)


def solution(mesh):
    space, tgt = mesh.shape["space"], mesh.shape["tgt"]
    chips = space // 2
    fine_mesh = Mesh(mesh.devices.reshape(chips, 2, tgt), ("chip", "core", "tgt"))
    every = ("chip", "core", "tgt")
    rows = ("chip", "core")
    placed = (
        P(every, None, None),
        P(every, None, None),
        P(every, None),
        P(every, None),
        P(),
        P(),
        P(rows, "tgt", None, None),
        P(rows, "tgt", None),
        P(rows, "tgt", None),
        P(rows, "tgt", None),
        P(rows, "tgt"),
    )
    return jax.shard_map(
        functools.partial(local, chips),
        mesh=fine_mesh,
        in_specs=placed,
        out_specs=(P(every, None, None), P(every, None, None)),
        check_vma=False,
    )
```

```python
import functools
import math

import jax
import jax.numpy as jnp
from jax import lax
from jax.experimental import pallas as pl
from jax.experimental.pallas import tpu as pltpu
from jax.sharding import Mesh
from jax.sharding import PartitionSpec as P

REG = 0.25
VMEM = pl.BlockSpec(memory_space=pltpu.VMEM)
HBM = pl.BlockSpec(memory_space=pltpu.HBM)
SMEM = pl.BlockSpec(memory_space=pltpu.SMEM)
VECTOR_CHUNKS = (2, 5, 8)
LIMIT = (2 << 20, 20 << 20, 20 << 20)


def ceil_to(n, m):
    return -(-n // m) * m


def iota(shape, dim):
    return lax.broadcasted_iota(jnp.int32, shape, dim)


def split3(x):
    high = x.astype(jnp.bfloat16).astype(jnp.float32)
    rest = x - high
    mid = rest.astype(jnp.bfloat16).astype(jnp.float32)
    low = (rest - mid).astype(jnp.bfloat16).astype(jnp.float32)
    return high, mid, low


def fetch_all(pairs, sems):
    copies = [
        pltpu.make_async_copy(src, dst, sems.at[i]) for i, (src, dst) in enumerate(pairs)
    ]
    for copy in copies:
        copy.start()
    return copies


def pack_kernel(
    nodes, send_hbm, pos_hbm, charge_hbm, weight_hbm, out_ref,
    send_ref, pos_ref, charge_ref, weight_ref, block, sems,
):
    copies = fetch_all(
        [
            (send_hbm, send_ref),
            (pos_hbm, pos_ref),
            (charge_hbm, charge_ref),
            (weight_hbm, weight_ref),
        ],
        sems,
    )
    lanes = block.shape[1]
    block[...] = jnp.zeros_like(block)
    for copy in copies:
        copy.wait()
    for c in range(3):
        block[c * 4 : (c + 1) * 4, 0:nodes] = pos_ref[c]
    block[12:16, 0:nodes] = charge_ref[...] * weight_ref[...]
    base = nodes - (lanes - 128)
    lane = iota((1, 128), 1)
    row = block[0:1, lanes - 128 : lanes]
    slots, shell = send_ref.shape
    for o in range(shell):
        for j in range(slots):
            row = jnp.where(
                lane == base + o * slots + j, send_ref[j, o].astype(jnp.float32), row
            )
    block[0:1, lanes - 128 : lanes] = row
    packed = block[...].astype(jnp.bfloat16)
    for i in range(out_ref.shape[0]):
        out_ref[i] = packed


def block_index(p, core):
    place = core + 4 - (p // 4) % 5
    return ((place // 2) * 8 + (place % 2) * 4 + p // 20) * 16


def select(hot, own_ref, side_ref, lo):
    total = None
    for i, ref in enumerate((side_ref.at[0], own_ref, side_ref.at[1])):
        blocks = ref[...]
        blocks = blocks.reshape(blocks.shape[0] * blocks.shape[1], blocks.shape[2])
        part = jnp.dot(
            hot[:, i * 128 : (i + 1) * 128],
            blocks[:, lo:],
            preferred_element_type=jnp.float32,
        )
        total = part if total is None else total + part
    return total


def inverse_cube(d):
    d = jnp.maximum(d.astype(jnp.bfloat16), jnp.bfloat16(REG))
    return lax.rsqrt(d * d * d)


def tile_slices(nodes):
    half = nodes // 2
    return [(0, half), (half, nodes)]


def target_kernel(
    count_ref, pos_hbm, slot_hbm, tile_hbm, applied_hbm, up_hbm, normal_hbm, weight_hbm,
    feat_ref, target_ref, mean_ref, wide_ref, head_ref, base_ref, want_ref, mask_ref,
    applied_ref, up_ref, normal_ref, weight_ref,
    pos_ref, slot_ref, tile_ref, ambient_ref, tiles, means, sems,
):
    copies = fetch_all(
        [
            (pos_hbm, pos_ref),
            (slot_hbm, slot_ref),
            (tile_hbm, tile_ref),
            (applied_hbm, ambient_ref),
            (up_hbm, up_ref),
            (normal_hbm, normal_ref),
            (weight_hbm, weight_ref),
        ],
        sems,
    )
    for copy in copies[:4]:
        copy.wait()
    core = lax.axis_index("core")
    pairs = slot_ref.shape[1]
    drops, nodes = pos_ref.shape[1:]
    half = nodes // 2
    wide = feat_ref.shape[1]

    height = head_ref.shape[0]
    row = iota((height, 128), 0)
    start = jnp.zeros((height, 128), jnp.int32)
    want = jnp.zeros((height, 128), jnp.int32)
    for k in range(pairs):
        p = slot_ref[0, k]
        start = jnp.where(row // 8 == k, block_index(p, core), start)
        want = jnp.where(row // 8 == k, nodes % 128 + p % 20, want)
    lane = iota((height, 128), 1)
    base_ref[...] = start + (row % 4) * 4
    want_ref[...] = want
    for i in range(3):
        head = (lane + i * 128 == start).astype(jnp.float32)
        head_ref[:, i * 128 : (i + 1) * 128] = head.astype(jnp.bfloat16)

    for c in range(3):
        applied_ref[c] = jnp.full(applied_ref.shape[1:], ambient_ref[0, c], jnp.float32)
    pair_id = iota((pairs, wide), 0)
    owner = jnp.full((pairs, wide), -1, jnp.int32)
    for k in range(pairs):
        mine = jnp.where(k < count_ref[0, 0], tile_ref[0, k], -1)
        owner = jnp.where(pair_id == k, mine, owner)
    for b in range(2 * drops):
        mask_ref[b] = (owner == b).astype(jnp.float32)

    tiles[...] = jnp.zeros_like(tiles)
    means[...] = jnp.zeros_like(means)
    for d in range(drops):
        for h, (lo, hi) in enumerate(tile_slices(nodes)):
            for c in range(3):
                line = pos_ref[c, d : d + 1, lo:hi]
                mean = jnp.sum(line, axis=1, keepdims=True) / half
                tiles[d * 2 + h, c : c + 1, 0:half] = line - mean
                means[d * 2 + h, c : c + 1, :] = jnp.broadcast_to(mean, (1, 128))
                means[d * 2 + h, c + 4 : c + 5, :] = jnp.broadcast_to(mean, (1, 128))
    sub = iota((8, wide), 0)
    part = iota((32, 512), 0)
    comp = iota((32, 512), 1) // 128
    coord = (part == comp) | (part == 8 + comp) | (part == 20 + comp)
    length = (part >= 24) & (part < 27)
    pick = ((comp < 3) & coord) | ((comp == 3) & length)
    pick = pick.astype(jnp.float32).astype(jnp.bfloat16)
    for k in range(pairs):
        b = tile_ref[0, k]
        t = tiles[b]
        target_ref[k] = t
        mean_ref[k] = means[b]
        norm = jnp.sum(t * t, axis=0, keepdims=True)
        t8 = jnp.where(sub < 4, t, jnp.concatenate([t[4:8], t[0:4]], axis=0))
        t8 = jnp.where(sub % 4 == 3, 1.0, t8)
        high, mid, low = split3(t8)
        nh, nm, nl = split3(norm)
        last = jnp.where(
            sub == 0, nh, jnp.where(sub == 1, nm, jnp.where(sub == 2, nl, 0.0))
        )
        stack = jnp.concatenate([high, mid, jnp.where(sub < 4, high, low), last], axis=0)
        feat_ref[k] = stack.T.astype(jnp.bfloat16)
        spread = jnp.dot(feat_ref[k], pick, preferred_element_type=jnp.float32)
        for c in range(4):
            wide_ref[k, c] = spread[:, c * 128 : (c + 1) * 128]
    for copy in copies[4:]:
        copy.wait()


def gather_tiles(values, mask_ref, b, rows):
    total = None
    for k in range(values.shape[0]):
        live = mask_ref[b, k : k + 1, :] > 0.5
        part = jnp.where(live, values[k, 0:rows, :], 0.0)
        total = part if total is None else total + part
    return total


def field_kernel(
    nodes,
    own_ref,
    side_ref,
    feats,
    targets,
    means,
    lanes_x,
    head_ref,
    base_ref,
    want_ref,
    mask_ref,
    applied_ref,
    up_ref,
    normal_ref,
    weight_ref,
    trac_ref,
    send_ref,
    cube_ref,
    hot_ref,
    fine_ref,
    block,
    values,
    field,
    src_a,
    src_b,
    coef_a,
    coef_b,
    row_a,
    row_b,
):
    pairs = values.shape[0]
    drops = weight_ref.shape[0]
    half = nodes // 2
    wide = feats.shape[1]
    fine_nodes = up_ref.shape[1]

    height = pairs * 8
    lane_id = iota((height, 128), 1)
    table = select(head_ref[...], own_ref, side_ref, nodes // 128 * 128)
    chosen = jnp.sum(
        jnp.where(lane_id == want_ref[...], table, 0.0), axis=1, keepdims=True
    )
    column = base_ref[...] + chosen.astype(jnp.int32)
    for i in range(3):
        hot = (lane_id + i * 128 == column).astype(jnp.float32)
        hot_ref[:, i * 128 : (i + 1) * 128] = hot.astype(jnp.bfloat16)
    picked = select(hot_ref[...], own_ref, side_ref, 0)
    fine = jnp.dot(
        picked[:, 0:nodes].astype(jnp.bfloat16),
        up_ref[...],
        preferred_element_type=jnp.float32,
    )
    for k in range(pairs):
        fine_ref[k] = fine[k * 8 : (k + 1) * 8]

    sub_f = iota((8, fine_nodes), 0)

    def prepare(k, src, coefs, qrow):
        f = fine_ref[k]
        charge = f[3:4]
        y = f - means[k, :, 0:1]
        y_only = jnp.where(sub_f < 3, y, 0.0)
        norm = jnp.sum(y_only * y_only, axis=0, keepdims=True) + REG
        q = jnp.where(sub_f % 4 == 3, norm, -2.0 * y)
        qrow[...] = q
        high, mid, low = split3(q)
        first = jnp.where(sub_f < 4, high, mid)
        second = jnp.where(sub_f < 4, low, high)
        third = jnp.where(sub_f < 3, 1.0, 0.0)
        src[...] = jnp.concatenate([first, first, second, third], axis=0).astype(jnp.bfloat16)
        coef = jnp.where(sub_f % 4 == 3, charge, charge * y)
        high, mid, low = split3(coef)
        coefs[...] = jnp.concatenate(
            [jnp.where(sub_f < 4, high, mid), jnp.where(sub_f < 4, low, 0.0)], axis=0
        ).astype(jnp.bfloat16)

    def work(k, src, coefs, qrow):
        tgt = feats[k]
        total = jnp.zeros((wide, 16), jnp.float32)
        for lo in range(0, fine_nodes, 256):
            hi = min(lo + 256, fine_nodes)
            if lo // 256 in VECTOR_CHUNKS:
                parts = []
                for at in range(lo, hi, 128):
                    end = min(at + 128, hi)
                    d = lanes_x[k, 3][:, : end - at] + qrow[3:4, at:end]
                    for c in range(3):
                        d = d + lanes_x[k, c][:, : end - at] * qrow[c : c + 1, at:end]
                    parts.append(inverse_cube(d))
                cube = jnp.concatenate(parts, axis=1) if len(parts) > 1 else parts[0]
            else:
                dist = jnp.dot(tgt, src[:, lo:hi], preferred_element_type=jnp.float32)
                cube = inverse_cube(dist)
            cube_ref[k, :, lo:hi] = cube
            total = total + lax.dot_general(
                cube,
                coefs[:, lo:hi],
                (((1,), (1,)), ((), ())),
                preferred_element_type=jnp.float32,
            )
        sums = total.T
        sums = sums[0:8] + sums[8:16]
        sums = sums + jnp.concatenate([sums[4:8], sums[0:4]], axis=0)
        values[k] = (targets[k] * sums[3:4] - sums) * (1.0 / (4.0 * math.pi))

    prepare(0, src_a, coef_a, row_a)

    def two(i, carry):
        k = 2 * i
        prepare(k + 1, src_b, coef_b, row_b)
        work(k, src_a, coef_a, row_a)
        prepare(jnp.minimum(k + 2, pairs - 1), src_a, coef_a, row_a)
        work(k + 1, src_b, coef_b, row_b)
        return carry

    lax.fori_loop(0, pairs // 2, two, 0)

    block[...] = jnp.zeros_like(block)
    for d in range(drops):
        for h, (lo, hi) in enumerate(tile_slices(nodes)):
            near = gather_tiles(values, mask_ref, d * 2 + h, 8)
            for c in range(3):
                field[c, d : d + 1, lo:hi] = near[c : c + 1, 0:half]
    e = [field[c] + applied_ref[c, :, 0:nodes] for c in range(3)]
    n = [normal_ref[c] for c in range(3)]
    along = e[0] * n[0] + e[1] * n[1] + e[2] * n[2]
    square = 0.5 * (e[0] * e[0] + e[1] * e[1] + e[2] * e[2])
    for c in range(3):
        t = along * e[c] - square * n[c]
        trac_ref[c] = t
        block[c * 4 : (c + 1) * 4, 0:nodes] = t * weight_ref[...]
    packed = block[...].astype(jnp.bfloat16)
    for i in range(send_ref.shape[0]):
        send_ref[i] = packed


def stokes_kernel(
    nodes,
    own_ref,
    side_ref,
    targets,
    means,
    mask_ref,
    up_ref,
    cube_ref,
    hot_ref,
    fine_ref,
    trac_ref,
    vel_ref,
    trac_hbm,
    forces,
    values,
    coef_a,
    coef_b,
    sems,
):
    copies = fetch_all([(trac_ref, trac_hbm)], sems)
    pairs = values.shape[0]
    drops = vel_ref.shape[1]
    half = nodes // 2
    fine_nodes = up_ref.shape[1]
    wide = targets.shape[2]

    picked = select(hot_ref[...], own_ref, side_ref, 0)
    fine = jnp.dot(
        picked[:, 0:nodes].astype(jnp.bfloat16),
        up_ref[...],
        preferred_element_type=jnp.float32,
    )
    for k in range(pairs):
        forces[k] = fine[k * 8 : (k + 1) * 8]

    sub_f = iota((8, fine_nodes), 0)

    def prepare(k, coefs):
        y = fine_ref[k] - means[k, :, 0:1]
        f = forces[k]
        y_only = jnp.where(sub_f < 3, y, 0.0)
        norm = jnp.sum(y_only * y_only, axis=0, keepdims=True)
        dot = jnp.sum(y_only * f, axis=0, keepdims=True)
        one = f * jnp.where(sub_f < 4, 1.0, norm)
        two = f * jnp.where(sub_f < 4, y[0:1], y[1:2])
        three = jnp.where(sub_f < 4, f * y[2:3], dot * y)
        parts = [split3(one), split3(two), split3(three)]
        coefs[...] = jnp.concatenate(
            [parts[g][s] for s in range(3) for g in range(3)]
            + [jnp.zeros((8, fine_nodes), jnp.float32)],
            axis=0,
        ).astype(jnp.bfloat16)

    def work(k, coefs):
        total = jnp.zeros((wide, 80), jnp.float32)
        for lo in range(0, fine_nodes, 256):
            hi = min(lo + 256, fine_nodes)
            total = total + lax.dot_general(
                cube_ref[k, :, lo:hi],
                coefs[:, lo:hi],
                (((1,), (1,)), ((), ())),
                preferred_element_type=jnp.float32,
            )
        sums = total.T
        sums = sums[0:24] + sums[24:48] + sums[48:72]
        x = targets[k][0:3]
        force, force_sq = sums[0:3], sums[4:7]
        t0, t1, t2 = sums[8:11], sums[12:15], sums[16:19]
        last = sums[20:23]
        x0, x1, x2 = x[0:1], x[1:2], x[2:3]
        square = x0 * x0 + x1 * x1 + x2 * x2
        trace = t0[0:1] + t1[1:2] + t2[2:3]
        reach = jnp.sum(x * force, axis=0, keepdims=True) - trace
        mixed = jnp.concatenate(
            [jnp.sum(x * t, axis=0, keepdims=True) for t in (t0, t1, t2)], axis=0
        )
        v = (square + 2.0 * REG) * force + force_sq
        v = v - 2.0 * (x0 * t0 + x1 * t1 + x2 * t2) + x * reach - mixed + last
        values[k, 0:3, :] = v * (1.0 / (8.0 * math.pi))

    prepare(0, coef_a)

    def two_pairs(i, carry):
        k = 2 * i
        prepare(k + 1, coef_b)
        work(k, coef_a)
        prepare(jnp.minimum(k + 2, pairs - 1), coef_a)
        work(k + 1, coef_b)
        return carry

    lax.fori_loop(0, pairs // 2, two_pairs, 0)
    for d in range(drops):
        for h, (lo, hi) in enumerate(tile_slices(nodes)):
            flow = gather_tiles(values, mask_ref, d * 2 + h, 3)
            for c in range(3):
                vel_ref[c, d : d + 1, lo:hi] = flow[c : c + 1, 0:half]
    copies[0].wait()


def exchange(mine, chips):
    own = lax.all_to_all(mine, ("core", "tgt"), 0, 0)
    moves = [(2 * i, 2 * i + 2) for i in range(chips - 1)]
    moves += [(2 * i + 3, 2 * i + 1) for i in range(chips - 1)]
    side = lax.ppermute(own, ("chip", "core"), moves)
    return own, side


def in_hbm(*arrays):
    return [pltpu.with_memory_space_constraint(a, pltpu.HBM) for a in arrays]


def share(side):
    return lax.all_gather(side, "core")


def local(
    chips,
    positions,
    normals,
    charge,
    weights,
    applied,
    upsample,
    send_list,
    send_count,
    pair_slot,
    pair_tile,
    pair_count,
):
    drops, _, nodes = positions.shape
    fine_nodes = upsample.shape[1]
    pairs = pair_slot.shape[2]
    lanes = ceil_to(nodes + 20, 128)
    wide = ceil_to(nodes // 2, 16)
    tiles = 2 * drops
    f32, bf16 = jnp.float32, jnp.bfloat16
    slots, tile_ids, count = pair_slot[0], pair_tile[0], pair_count

    positions = positions.transpose(1, 0, 2)
    normals = normals.transpose(1, 0, 2)

    i32 = jnp.int32
    dma = pltpu.SemaphoreType.DMA
    mine = pl.pallas_call(
        functools.partial(pack_kernel, nodes),
        out_shape=jax.ShapeDtypeStruct((8, 16, lanes), bf16),
        in_specs=[HBM] * 4,
        out_specs=VMEM,
        scratch_shapes=[
            pltpu.SMEM(send_list.shape[:1:-1], i32),
            pltpu.VMEM((3, drops, nodes), f32),
            pltpu.VMEM((drops, nodes), f32),
            pltpu.VMEM((drops, nodes), f32),
            pltpu.VMEM((16, lanes), f32),
            dma((4,)),
        ],
        compiler_params=pltpu.CompilerParams(vmem_limit_bytes=LIMIT[0]),
        name="pack",
    )(*in_hbm(send_list[0, 0].T, positions, charge, weights))
    own, side = exchange(mine, chips)

    shape = jax.ShapeDtypeStruct
    info = pl.pallas_call(
        target_kernel,
        out_shape=(
            shape((pairs, wide, 32), bf16),
            shape((pairs, 8, wide), f32),
            shape((pairs, 8, 128), f32),
            shape((pairs, 4, wide, 128), f32),
            shape((pairs * 8, 384), bf16),
            shape((pairs * 8, 128), i32),
            shape((pairs * 8, 128), i32),
            shape((tiles, pairs, wide), f32),
            shape((3, drops, lanes), f32),
            shape(upsample.shape, bf16),
            shape((3, drops, nodes), f32),
            shape((drops, nodes), f32),
        ),
        in_specs=[SMEM] + [HBM] * 7,
        out_specs=(VMEM,) * 12,
        scratch_shapes=[
            pltpu.VMEM((3, drops, nodes), f32),
            pltpu.SMEM((1, pairs), i32),
            pltpu.SMEM((1, pairs), i32),
            pltpu.SMEM((1, 3), f32),
            pltpu.VMEM((tiles, 8, wide), f32),
            pltpu.VMEM((tiles, 8, 128), f32),
            dma((7,)),
        ],
        compiler_params=pltpu.CompilerParams(vmem_limit_bytes=LIMIT[0]),
        cost_estimate=pl.CostEstimate(
            flops=4_000_000, bytes_accessed=6_000_000, transcendentals=0
        ),
        name="target",
    )(count, *in_hbm(positions, slots, tile_ids, applied[None], upsample, normals, weights))
    targets, means, mask, up = info[1], info[2], info[7], info[9]

    traction, forces, cubes, hot, fine = pl.pallas_call(
        functools.partial(field_kernel, nodes),
        out_shape=(
            shape((3, drops, nodes), f32),
            shape((8, 16, lanes), bf16),
            shape((pairs, wide, fine_nodes), bf16),
            shape((pairs * 8, 384), bf16),
            shape((pairs, 8, fine_nodes), f32),
        ),
        in_specs=[VMEM] * 14,
        out_specs=(VMEM,) * 5,
        scratch_shapes=[
            pltpu.VMEM((16, lanes), f32),
            pltpu.VMEM((pairs, 8, wide), f32),
            pltpu.VMEM((3, drops, nodes), f32),
            pltpu.VMEM((32, fine_nodes), bf16),
            pltpu.VMEM((32, fine_nodes), bf16),
            pltpu.VMEM((16, fine_nodes), bf16),
            pltpu.VMEM((16, fine_nodes), bf16),
            pltpu.VMEM((8, fine_nodes), f32),
            pltpu.VMEM((8, fine_nodes), f32),
        ],
        compiler_params=pltpu.CompilerParams(vmem_limit_bytes=LIMIT[1]),
        name="field",
    )(own, share(side), *info)
    own, side = exchange(forces, chips)

    velocity, traction = pl.pallas_call(
        functools.partial(stokes_kernel, nodes),
        out_shape=(shape((3, drops, nodes), f32),) * 2,
        in_specs=[VMEM] * 10,
        out_specs=(VMEM, HBM),
        scratch_shapes=[
            pltpu.VMEM((pairs, 8, fine_nodes), f32),
            pltpu.VMEM((pairs, 8, wide), f32),
            pltpu.VMEM((80, fine_nodes), bf16),
            pltpu.VMEM((80, fine_nodes), bf16),
            dma((1,)),
        ],
        compiler_params=pltpu.CompilerParams(vmem_limit_bytes=LIMIT[2]),
        name="stokes",
    )(own, share(side), targets, means, mask, up, cubes, hot, fine, traction)
    return traction.transpose(1, 0, 2), velocity.transpose(1, 0, 2)


def solution(mesh):
    space, tgt = mesh.shape["space"], mesh.shape["tgt"]
    chips = space // 2
    fine_mesh = Mesh(mesh.devices.reshape(chips, 2, tgt), ("chip", "core", "tgt"))
    every = ("chip", "core", "tgt")
    rows = ("chip", "core")
    placed = (
        P(every, None, None),
        P(every, None, None),
        P(every, None),
        P(every, None),
        P(),
        P(),
        P(rows, "tgt", None, None),
        P(rows, "tgt", None),
        P(rows, "tgt", None),
        P(rows, "tgt", None),
        P(rows, "tgt"),
    )
    return jax.shard_map(
        functools.partial(local, chips),
        mesh=fine_mesh,
        in_specs=placed,
        out_specs=(P(every, None, None), P(every, None, None)),
        check_vma=False,
    )
```

```python
import functools
import math

import jax
import jax.numpy as jnp
from jax import lax
from jax.experimental import pallas as pl
from jax.experimental.pallas import tpu as pltpu
from jax.sharding import Mesh
from jax.sharding import PartitionSpec as P

REG = 0.25
VMEM = pl.BlockSpec(memory_space=pltpu.VMEM)
HBM = pl.BlockSpec(memory_space=pltpu.HBM)
SMEM = pl.BlockSpec(memory_space=pltpu.SMEM)
VECTOR_CHUNKS = (7, 8)
LIMIT = (2 << 20, 20 << 20, 20 << 20)


def ceil_to(n, m):
    return -(-n // m) * m


def iota(shape, dim):
    return lax.broadcasted_iota(jnp.int32, shape, dim)


def split3(x):
    high = x.astype(jnp.bfloat16).astype(jnp.float32)
    rest = x - high
    mid = rest.astype(jnp.bfloat16).astype(jnp.float32)
    low = (rest - mid).astype(jnp.bfloat16).astype(jnp.float32)
    return high, mid, low


def fetch_all(pairs, sems):
    copies = [
        pltpu.make_async_copy(src, dst, sems.at[i]) for i, (src, dst) in enumerate(pairs)
    ]
    for copy in copies:
        copy.start()
    return copies


def pack_kernel(
    nodes, send_hbm, pos_hbm, charge_hbm, weight_hbm, out_ref,
    send_ref, pos_ref, charge_ref, weight_ref, block, sems,
):
    copies = fetch_all(
        [
            (send_hbm, send_ref),
            (pos_hbm, pos_ref),
            (charge_hbm, charge_ref),
            (weight_hbm, weight_ref),
        ],
        sems,
    )
    lanes = block.shape[1]
    block[...] = jnp.zeros_like(block)
    for copy in copies:
        copy.wait()
    for c in range(3):
        block[c * 4 : (c + 1) * 4, 0:nodes] = pos_ref[c]
    block[12:16, 0:nodes] = charge_ref[...] * weight_ref[...]
    base = nodes - (lanes - 128)
    lane = iota((1, 128), 1)
    row = block[0:1, lanes - 128 : lanes]
    slots, shell = send_ref.shape
    for o in range(shell):
        for j in range(slots):
            row = jnp.where(
                lane == base + o * slots + j, send_ref[j, o].astype(jnp.float32), row
            )
    block[0:1, lanes - 128 : lanes] = row
    packed = block[...].astype(jnp.bfloat16)
    for i in range(out_ref.shape[0]):
        out_ref[i] = packed


def block_index(p, core):
    place = core + 4 - (p // 4) % 5
    return ((place // 2) * 8 + (place % 2) * 4 + p // 20) * 16


def select(hot, own_ref, side_ref, lo):
    total = None
    for i, ref in enumerate((side_ref.at[0], own_ref, side_ref.at[1])):
        blocks = ref[...]
        blocks = blocks.reshape(blocks.shape[0] * blocks.shape[1], blocks.shape[2])
        part = jnp.dot(
            hot[:, i * 128 : (i + 1) * 128],
            blocks[:, lo:],
            preferred_element_type=jnp.float32,
        )
        total = part if total is None else total + part
    return total


def inverse_cube(d):
    d = jnp.maximum(d.astype(jnp.bfloat16), jnp.bfloat16(REG))
    return lax.rsqrt(d * d * d)


def tile_slices(nodes):
    half = nodes // 2
    return [(0, half), (half, nodes)]


def target_kernel(
    count_ref, pos_hbm, slot_hbm, tile_hbm, applied_hbm, up_hbm, normal_hbm, weight_hbm,
    feat_ref, target_ref, mean_ref, wide_ref, head_ref, base_ref, want_ref, mask_ref,
    applied_ref, up_ref, normal_ref, weight_ref,
    pos_ref, slot_ref, tile_ref, ambient_ref, tiles, means, sems,
):
    copies = fetch_all(
        [
            (pos_hbm, pos_ref),
            (slot_hbm, slot_ref),
            (tile_hbm, tile_ref),
            (applied_hbm, ambient_ref),
            (up_hbm, up_ref),
            (normal_hbm, normal_ref),
            (weight_hbm, weight_ref),
        ],
        sems,
    )
    for copy in copies[:4]:
        copy.wait()
    core = lax.axis_index("core")
    pairs = slot_ref.shape[1]
    drops, nodes = pos_ref.shape[1:]
    half = nodes // 2
    wide = feat_ref.shape[1]

    height = head_ref.shape[0]
    row = iota((height, 128), 0)
    start = jnp.zeros((height, 128), jnp.int32)
    want = jnp.zeros((height, 128), jnp.int32)
    for k in range(pairs):
        p = slot_ref[0, k]
        start = jnp.where(row // 8 == k, block_index(p, core), start)
        want = jnp.where(row // 8 == k, nodes % 128 + p % 20, want)
    lane = iota((height, 128), 1)
    base_ref[...] = start + (row % 4) * 4
    want_ref[...] = want
    for i in range(3):
        head = (lane + i * 128 == start).astype(jnp.float32)
        head_ref[:, i * 128 : (i + 1) * 128] = head.astype(jnp.bfloat16)

    for c in range(3):
        applied_ref[c] = jnp.full(applied_ref.shape[1:], ambient_ref[0, c], jnp.float32)
    pair_id = iota((pairs, wide), 0)
    owner = jnp.full((pairs, wide), -1, jnp.int32)
    for k in range(pairs):
        mine = jnp.where(k < count_ref[0, 0], tile_ref[0, k], -1)
        owner = jnp.where(pair_id == k, mine, owner)
    for b in range(2 * drops):
        mask_ref[b] = (owner == b).astype(jnp.float32)

    tiles[...] = jnp.zeros_like(tiles)
    means[...] = jnp.zeros_like(means)
    for d in range(drops):
        for h, (lo, hi) in enumerate(tile_slices(nodes)):
            for c in range(3):
                line = pos_ref[c, d : d + 1, lo:hi]
                mean = jnp.sum(line, axis=1, keepdims=True) / half
                tiles[d * 2 + h, c : c + 1, 0:half] = line - mean
                means[d * 2 + h, c : c + 1, :] = jnp.broadcast_to(mean, (1, 128))
                means[d * 2 + h, c + 4 : c + 5, :] = jnp.broadcast_to(mean, (1, 128))
    sub = iota((8, wide), 0)
    part = iota((32, 512), 0)
    comp = iota((32, 512), 1) // 128
    coord = (part == comp) | (part == 8 + comp) | (part == 20 + comp)
    length = (part >= 24) & (part < 27)
    pick = ((comp < 3) & coord) | ((comp == 3) & length)
    pick = pick.astype(jnp.float32).astype(jnp.bfloat16)
    for k in range(pairs):
        b = tile_ref[0, k]
        t = tiles[b]
        target_ref[k] = t
        mean_ref[k] = means[b]
        norm = jnp.sum(t * t, axis=0, keepdims=True)
        t8 = jnp.where(sub < 4, t, jnp.concatenate([t[4:8], t[0:4]], axis=0))
        t8 = jnp.where(sub % 4 == 3, 1.0, t8)
        high, mid, low = split3(t8)
        nh, nm, nl = split3(norm)
        last = jnp.where(
            sub == 0, nh, jnp.where(sub == 1, nm, jnp.where(sub == 2, nl, 0.0))
        )
        stack = jnp.concatenate([high, mid, jnp.where(sub < 4, high, low), last], axis=0)
        feat_ref[k] = stack.T.astype(jnp.bfloat16)
        spread = jnp.dot(feat_ref[k], pick, preferred_element_type=jnp.float32)
        for c in range(4):
            wide_ref[k, c] = spread[:, c * 128 : (c + 1) * 128]
    for copy in copies[4:]:
        copy.wait()


def gather_tiles(values, mask_ref, b, rows):
    total = None
    for k in range(values.shape[0]):
        live = mask_ref[b, k : k + 1, :] > 0.5
        part = jnp.where(live, values[k, 0:rows, :], 0.0)
        total = part if total is None else total + part
    return total


def field_kernel(
    nodes,
    own_ref,
    side_ref,
    feats,
    targets,
    means,
    lanes_x,
    head_ref,
    base_ref,
    want_ref,
    mask_ref,
    applied_ref,
    up_ref,
    normal_ref,
    weight_ref,
    trac_ref,
    send_ref,
    cube_ref,
    hot_ref,
    fine_ref,
    block,
    values,
    field,
    src_a,
    src_b,
    coef_a,
    coef_b,
    row_a,
    row_b,
):
    pairs = values.shape[0]
    drops = weight_ref.shape[0]
    half = nodes // 2
    wide = feats.shape[1]
    fine_nodes = up_ref.shape[1]

    height = pairs * 8
    lane_id = iota((height, 128), 1)
    table = select(head_ref[...], own_ref, side_ref, nodes // 128 * 128)
    chosen = jnp.sum(
        jnp.where(lane_id == want_ref[...], table, 0.0), axis=1, keepdims=True
    )
    column = base_ref[...] + chosen.astype(jnp.int32)
    for i in range(3):
        hot = (lane_id + i * 128 == column).astype(jnp.float32)
        hot_ref[:, i * 128 : (i + 1) * 128] = hot.astype(jnp.bfloat16)
    picked = select(hot_ref[...], own_ref, side_ref, 0)
    fine = jnp.dot(
        picked[:, 0:nodes].astype(jnp.bfloat16),
        up_ref[...],
        preferred_element_type=jnp.float32,
    )
    for k in range(pairs):
        fine_ref[k] = fine[k * 8 : (k + 1) * 8]

    sub_f = iota((8, fine_nodes), 0)

    def prepare(k, src, coefs, qrow):
        f = fine_ref[k]
        charge = f[3:4]
        y = f - means[k, :, 0:1]
        y_only = jnp.where(sub_f < 3, y, 0.0)
        norm = jnp.sum(y_only * y_only, axis=0, keepdims=True) + REG
        q = jnp.where(sub_f % 4 == 3, norm, -2.0 * y)
        qrow[...] = q
        high, mid, low = split3(q)
        first = jnp.where(sub_f < 4, high, mid)
        second = jnp.where(sub_f < 4, low, high)
        third = jnp.where(sub_f < 3, 1.0, 0.0)
        src[...] = jnp.concatenate([first, first, second, third], axis=0).astype(jnp.bfloat16)
        coef = jnp.where(sub_f % 4 == 3, charge, charge * y)
        high, mid, low = split3(coef)
        coefs[...] = jnp.concatenate(
            [jnp.where(sub_f < 4, high, mid), jnp.where(sub_f < 4, low, 0.0)], axis=0
        ).astype(jnp.bfloat16)

    def work(k, src, coefs, qrow):
        tgt = feats[k]
        cubes = []
        for lo in range(0, fine_nodes, 256):
            hi = min(lo + 256, fine_nodes)
            if lo // 256 in VECTOR_CHUNKS:
                parts = []
                for at in range(lo, hi, 128):
                    end = min(at + 128, hi)
                    d = lanes_x[k, 3][:, : end - at] + qrow[3:4, at:end]
                    for c in range(3):
                        d = d + lanes_x[k, c][:, : end - at] * qrow[c : c + 1, at:end]
                    parts.append(inverse_cube(d))
                cube = jnp.concatenate(parts, axis=1) if len(parts) > 1 else parts[0]
            else:
                dist = jnp.dot(tgt, src[:, lo:hi], preferred_element_type=jnp.float32)
                cube = inverse_cube(dist)
            cube_ref[k, :, lo:hi] = cube
            cubes.append(cube)
        total = lax.dot_general(
            jnp.concatenate(cubes, axis=1),
            coefs[...],
            (((1,), (1,)), ((), ())),
            preferred_element_type=jnp.float32,
        )
        sums = total.T
        sums = sums[0:8] + sums[8:16]
        sums = sums + jnp.concatenate([sums[4:8], sums[0:4]], axis=0)
        values[k] = (targets[k] * sums[3:4] - sums) * (1.0 / (4.0 * math.pi))

    prepare(0, src_a, coef_a, row_a)

    def two(i, carry):
        k = 2 * i
        prepare(k + 1, src_b, coef_b, row_b)
        work(k, src_a, coef_a, row_a)
        prepare(jnp.minimum(k + 2, pairs - 1), src_a, coef_a, row_a)
        work(k + 1, src_b, coef_b, row_b)
        return carry

    lax.fori_loop(0, pairs // 2, two, 0)

    block[...] = jnp.zeros_like(block)
    for d in range(drops):
        for h, (lo, hi) in enumerate(tile_slices(nodes)):
            near = gather_tiles(values, mask_ref, d * 2 + h, 8)
            for c in range(3):
                field[c, d : d + 1, lo:hi] = near[c : c + 1, 0:half]
    e = [field[c] + applied_ref[c, :, 0:nodes] for c in range(3)]
    n = [normal_ref[c] for c in range(3)]
    along = e[0] * n[0] + e[1] * n[1] + e[2] * n[2]
    square = 0.5 * (e[0] * e[0] + e[1] * e[1] + e[2] * e[2])
    for c in range(3):
        t = along * e[c] - square * n[c]
        trac_ref[c] = t
        block[c * 4 : (c + 1) * 4, 0:nodes] = t * weight_ref[...]
    packed = block[...].astype(jnp.bfloat16)
    for i in range(send_ref.shape[0]):
        send_ref[i] = packed


def stokes_kernel(
    nodes,
    own_ref,
    side_ref,
    targets,
    means,
    mask_ref,
    up_ref,
    cube_ref,
    hot_ref,
    fine_ref,
    trac_ref,
    vel_ref,
    trac_hbm,
    forces,
    values,
    coef_a,
    coef_b,
    sems,
):
    copies = fetch_all([(trac_ref, trac_hbm)], sems)
    pairs = values.shape[0]
    drops = vel_ref.shape[1]
    half = nodes // 2
    fine_nodes = up_ref.shape[1]
    wide = targets.shape[2]

    picked = select(hot_ref[...], own_ref, side_ref, 0)
    fine = jnp.dot(
        picked[:, 0:nodes].astype(jnp.bfloat16),
        up_ref[...],
        preferred_element_type=jnp.float32,
    )
    for k in range(pairs):
        forces[k] = fine[k * 8 : (k + 1) * 8]

    sub_f = iota((8, fine_nodes), 0)

    def prepare(k, coefs):
        y = fine_ref[k] - means[k, :, 0:1]
        f = forces[k]
        y_only = jnp.where(sub_f < 3, y, 0.0)
        norm = jnp.sum(y_only * y_only, axis=0, keepdims=True)
        dot = jnp.sum(y_only * f, axis=0, keepdims=True)
        one = f * jnp.where(sub_f < 4, 1.0, norm)
        two = f * jnp.where(sub_f < 4, y[0:1], y[1:2])
        three = jnp.where(sub_f < 4, f * y[2:3], dot * y)
        parts = [split3(one), split3(two), split3(three)]
        coefs[...] = jnp.concatenate(
            [parts[g][s] for s in range(3) for g in range(3)]
            + [jnp.zeros((8, fine_nodes), jnp.float32)],
            axis=0,
        ).astype(jnp.bfloat16)

    def work(k, coefs):
        total = jnp.zeros((wide, 80), jnp.float32)
        for lo in range(0, fine_nodes, 256):
            hi = min(lo + 256, fine_nodes)
            total = total + lax.dot_general(
                cube_ref[k, :, lo:hi],
                coefs[:, lo:hi],
                (((1,), (1,)), ((), ())),
                preferred_element_type=jnp.float32,
            )
        sums = total.T
        sums = sums[0:24] + sums[24:48] + sums[48:72]
        x = targets[k][0:3]
        force, force_sq = sums[0:3], sums[4:7]
        t0, t1, t2 = sums[8:11], sums[12:15], sums[16:19]
        last = sums[20:23]
        x0, x1, x2 = x[0:1], x[1:2], x[2:3]
        square = x0 * x0 + x1 * x1 + x2 * x2
        trace = t0[0:1] + t1[1:2] + t2[2:3]
        reach = jnp.sum(x * force, axis=0, keepdims=True) - trace
        mixed = jnp.concatenate(
            [jnp.sum(x * t, axis=0, keepdims=True) for t in (t0, t1, t2)], axis=0
        )
        v = (square + 2.0 * REG) * force + force_sq
        v = v - 2.0 * (x0 * t0 + x1 * t1 + x2 * t2) + x * reach - mixed + last
        values[k, 0:3, :] = v * (1.0 / (8.0 * math.pi))

    prepare(0, coef_a)

    def two_pairs(i, carry):
        k = 2 * i
        prepare(k + 1, coef_b)
        work(k, coef_a)
        prepare(jnp.minimum(k + 2, pairs - 1), coef_a)
        work(k + 1, coef_b)
        return carry

    lax.fori_loop(0, pairs // 2, two_pairs, 0)
    for d in range(drops):
        for h, (lo, hi) in enumerate(tile_slices(nodes)):
            flow = gather_tiles(values, mask_ref, d * 2 + h, 3)
            for c in range(3):
                vel_ref[c, d : d + 1, lo:hi] = flow[c : c + 1, 0:half]
    copies[0].wait()


def exchange(mine, chips):
    own = lax.all_to_all(mine, ("core", "tgt"), 0, 0)
    moves = [(2 * i, 2 * i + 2) for i in range(chips - 1)]
    moves += [(2 * i + 3, 2 * i + 1) for i in range(chips - 1)]
    side = lax.ppermute(own, ("chip", "core"), moves)
    return own, side


def in_hbm(*arrays):
    return [pltpu.with_memory_space_constraint(a, pltpu.HBM) for a in arrays]


def share(side):
    return lax.all_gather(side, "core")


def local(
    chips,
    positions,
    normals,
    charge,
    weights,
    applied,
    upsample,
    send_list,
    send_count,
    pair_slot,
    pair_tile,
    pair_count,
):
    drops, _, nodes = positions.shape
    fine_nodes = upsample.shape[1]
    pairs = pair_slot.shape[2]
    lanes = ceil_to(nodes + 20, 128)
    wide = ceil_to(nodes // 2, 16)
    tiles = 2 * drops
    f32, bf16 = jnp.float32, jnp.bfloat16
    slots, tile_ids, count = pair_slot[0], pair_tile[0], pair_count

    positions = positions.transpose(1, 0, 2)
    normals = normals.transpose(1, 0, 2)

    i32 = jnp.int32
    dma = pltpu.SemaphoreType.DMA
    mine = pl.pallas_call(
        functools.partial(pack_kernel, nodes),
        out_shape=jax.ShapeDtypeStruct((8, 16, lanes), bf16),
        in_specs=[HBM] * 4,
        out_specs=VMEM,
        scratch_shapes=[
            pltpu.SMEM(send_list.shape[:1:-1], i32),
            pltpu.VMEM((3, drops, nodes), f32),
            pltpu.VMEM((drops, nodes), f32),
            pltpu.VMEM((drops, nodes), f32),
            pltpu.VMEM((16, lanes), f32),
            dma((4,)),
        ],
        compiler_params=pltpu.CompilerParams(vmem_limit_bytes=LIMIT[0]),
        name="pack",
    )(*in_hbm(send_list[0, 0].T, positions, charge, weights))
    own, side = exchange(mine, chips)

    shape = jax.ShapeDtypeStruct
    info = pl.pallas_call(
        target_kernel,
        out_shape=(
            shape((pairs, wide, 32), bf16),
            shape((pairs, 8, wide), f32),
            shape((pairs, 8, 128), f32),
            shape((pairs, 4, wide, 128), f32),
            shape((pairs * 8, 384), bf16),
            shape((pairs * 8, 128), i32),
            shape((pairs * 8, 128), i32),
            shape((tiles, pairs, wide), f32),
            shape((3, drops, lanes), f32),
            shape(upsample.shape, bf16),
            shape((3, drops, nodes), f32),
            shape((drops, nodes), f32),
        ),
        in_specs=[SMEM] + [HBM] * 7,
        out_specs=(VMEM,) * 12,
        scratch_shapes=[
            pltpu.VMEM((3, drops, nodes), f32),
            pltpu.SMEM((1, pairs), i32),
            pltpu.SMEM((1, pairs), i32),
            pltpu.SMEM((1, 3), f32),
            pltpu.VMEM((tiles, 8, wide), f32),
            pltpu.VMEM((tiles, 8, 128), f32),
            dma((7,)),
        ],
        compiler_params=pltpu.CompilerParams(vmem_limit_bytes=LIMIT[0]),
        cost_estimate=pl.CostEstimate(
            flops=4_000_000, bytes_accessed=6_000_000, transcendentals=0
        ),
        name="target",
    )(count, *in_hbm(positions, slots, tile_ids, applied[None], upsample, normals, weights))
    targets, means, mask, up = info[1], info[2], info[7], info[9]

    traction, forces, cubes, hot, fine = pl.pallas_call(
        functools.partial(field_kernel, nodes),
        out_shape=(
            shape((3, drops, nodes), f32),
            shape((8, 16, lanes), bf16),
            shape((pairs, wide, fine_nodes), bf16),
            shape((pairs * 8, 384), bf16),
            shape((pairs, 8, fine_nodes), f32),
        ),
        in_specs=[VMEM] * 14,
        out_specs=(VMEM,) * 5,
        scratch_shapes=[
            pltpu.VMEM((16, lanes), f32),
            pltpu.VMEM((pairs, 8, wide), f32),
            pltpu.VMEM((3, drops, nodes), f32),
            pltpu.VMEM((32, fine_nodes), bf16),
            pltpu.VMEM((32, fine_nodes), bf16),
            pltpu.VMEM((16, fine_nodes), bf16),
            pltpu.VMEM((16, fine_nodes), bf16),
            pltpu.VMEM((8, fine_nodes), f32),
            pltpu.VMEM((8, fine_nodes), f32),
        ],
        compiler_params=pltpu.CompilerParams(vmem_limit_bytes=LIMIT[1]),
        name="field",
    )(own, share(side), *info)
    own, side = exchange(forces, chips)

    velocity, traction = pl.pallas_call(
        functools.partial(stokes_kernel, nodes),
        out_shape=(shape((3, drops, nodes), f32),) * 2,
        in_specs=[VMEM] * 10,
        out_specs=(VMEM, HBM),
        scratch_shapes=[
            pltpu.VMEM((pairs, 8, fine_nodes), f32),
            pltpu.VMEM((pairs, 8, wide), f32),
            pltpu.VMEM((80, fine_nodes), bf16),
            pltpu.VMEM((80, fine_nodes), bf16),
            dma((1,)),
        ],
        compiler_params=pltpu.CompilerParams(vmem_limit_bytes=LIMIT[2]),
        name="stokes",
    )(own, share(side), targets, means, mask, up, cubes, hot, fine, traction)
    return traction.transpose(1, 0, 2), velocity.transpose(1, 0, 2)


def solution(mesh):
    space, tgt = mesh.shape["space"], mesh.shape["tgt"]
    chips = space // 2
    fine_mesh = Mesh(mesh.devices.reshape(chips, 2, tgt), ("chip", "core", "tgt"))
    every = ("chip", "core", "tgt")
    rows = ("chip", "core")
    placed = (
        P(every, None, None),
        P(every, None, None),
        P(every, None),
        P(every, None),
        P(),
        P(),
        P(rows, "tgt", None, None),
        P(rows, "tgt", None),
        P(rows, "tgt", None),
        P(rows, "tgt", None),
        P(rows, "tgt"),
    )
    return jax.shard_map(
        functools.partial(local, chips),
        mesh=fine_mesh,
        in_specs=placed,
        out_specs=(P(every, None, None), P(every, None, None)),
        check_vma=False,
    )
```

```python
import functools
import math

import jax
import jax.numpy as jnp
from jax import lax
from jax.experimental import pallas as pl
from jax.experimental.pallas import tpu as pltpu
from jax.sharding import Mesh
from jax.sharding import PartitionSpec as P

REG = 0.25
VMEM = pl.BlockSpec(memory_space=pltpu.VMEM)
HBM = pl.BlockSpec(memory_space=pltpu.HBM)
SMEM = pl.BlockSpec(memory_space=pltpu.SMEM)
VECTOR_CHUNKS = (7, 8)
LIMIT = (2 << 20, 20 << 20, 20 << 20)


def ceil_to(n, m):
    return -(-n // m) * m


def iota(shape, dim):
    return lax.broadcasted_iota(jnp.int32, shape, dim)


def split3(x):
    high = x.astype(jnp.bfloat16).astype(jnp.float32)
    rest = x - high
    mid = rest.astype(jnp.bfloat16).astype(jnp.float32)
    low = (rest - mid).astype(jnp.bfloat16).astype(jnp.float32)
    return high, mid, low


def fetch_all(pairs, sems):
    copies = [
        pltpu.make_async_copy(src, dst, sems.at[i]) for i, (src, dst) in enumerate(pairs)
    ]
    for copy in copies:
        copy.start()
    return copies


def pack_kernel(
    nodes, send_hbm, pos_hbm, charge_hbm, weight_hbm, out_ref,
    send_ref, pos_ref, charge_ref, weight_ref, block, sems,
):
    copies = fetch_all(
        [
            (send_hbm, send_ref),
            (pos_hbm, pos_ref),
            (charge_hbm, charge_ref),
            (weight_hbm, weight_ref),
        ],
        sems,
    )
    lanes = block.shape[1]
    block[...] = jnp.zeros_like(block)
    for copy in copies:
        copy.wait()
    for c in range(3):
        block[c * 4 : (c + 1) * 4, 0:nodes] = pos_ref[c]
    block[12:16, 0:nodes] = charge_ref[...] * weight_ref[...]
    base = nodes - (lanes - 128)
    lane = iota((1, 128), 1)
    row = block[0:1, lanes - 128 : lanes]
    slots, shell = send_ref.shape
    for o in range(shell):
        for j in range(slots):
            row = jnp.where(
                lane == base + o * slots + j, send_ref[j, o].astype(jnp.float32), row
            )
    block[0:1, lanes - 128 : lanes] = row
    packed = block[...].astype(jnp.bfloat16)
    for i in range(out_ref.shape[0]):
        out_ref[i] = packed


def block_index(p, core):
    place = core + 4 - (p // 4) % 5
    return ((place // 2) * 8 + (place % 2) * 4 + p // 20) * 16


def select(hot, own_ref, side_ref, lo):
    total = None
    for i, ref in enumerate((side_ref.at[0], own_ref, side_ref.at[1])):
        blocks = ref[...]
        blocks = blocks.reshape(blocks.shape[0] * blocks.shape[1], blocks.shape[2])
        part = jnp.dot(
            hot[:, i * 128 : (i + 1) * 128],
            blocks[:, lo:],
            preferred_element_type=jnp.float32,
        )
        total = part if total is None else total + part
    return total


def inverse_cube(d):
    d = jnp.maximum(d.astype(jnp.bfloat16), jnp.bfloat16(REG))
    return lax.rsqrt(d * d * d)


def tile_slices(nodes):
    half = nodes // 2
    return [(0, half), (half, nodes)]


def target_kernel(
    count_ref, pos_hbm, slot_hbm, tile_hbm, applied_hbm, up_hbm, normal_hbm, weight_hbm,
    feat_ref, target_ref, mean_ref, wide_ref, head_ref, base_ref, want_ref, mask_ref,
    applied_ref, up_ref, normal_ref, weight_ref,
    pos_ref, slot_ref, tile_ref, ambient_ref, tiles, means, sems,
):
    copies = fetch_all(
        [
            (pos_hbm, pos_ref),
            (slot_hbm, slot_ref),
            (tile_hbm, tile_ref),
            (applied_hbm, ambient_ref),
            (up_hbm, up_ref),
            (normal_hbm, normal_ref),
            (weight_hbm, weight_ref),
        ],
        sems,
    )
    for copy in copies[:4]:
        copy.wait()
    core = lax.axis_index("core")
    pairs = slot_ref.shape[1]
    drops, nodes = pos_ref.shape[1:]
    half = nodes // 2
    wide = feat_ref.shape[1]

    height = head_ref.shape[0]
    row = iota((height, 128), 0)
    start = jnp.zeros((height, 128), jnp.int32)
    want = jnp.zeros((height, 128), jnp.int32)
    for k in range(pairs):
        p = slot_ref[0, k]
        start = jnp.where(row // 4 == k, block_index(p, core), start)
        want = jnp.where(row // 4 == k, nodes % 128 + p % 20, want)
    lane = iota((height, 128), 1)
    base_ref[...] = start + (row % 4) * 4
    want_ref[...] = want
    for i in range(3):
        head = (lane + i * 128 == start).astype(jnp.float32)
        head_ref[:, i * 128 : (i + 1) * 128] = head.astype(jnp.bfloat16)

    for c in range(3):
        applied_ref[c] = jnp.full(applied_ref.shape[1:], ambient_ref[0, c], jnp.float32)
    pair_id = iota((pairs, wide), 0)
    owner = jnp.full((pairs, wide), -1, jnp.int32)
    for k in range(pairs):
        mine = jnp.where(k < count_ref[0, 0], tile_ref[0, k], -1)
        owner = jnp.where(pair_id == k, mine, owner)
    for b in range(2 * drops):
        mask_ref[b] = (owner == b).astype(jnp.float32)

    tiles[...] = jnp.zeros_like(tiles)
    means[...] = jnp.zeros_like(means)
    for d in range(drops):
        for h, (lo, hi) in enumerate(tile_slices(nodes)):
            for c in range(3):
                line = pos_ref[c, d : d + 1, lo:hi]
                mean = jnp.sum(line, axis=1, keepdims=True) / half
                tiles[d * 2 + h, c : c + 1, 0:half] = line - mean
                means[d * 2 + h, c : c + 1, :] = jnp.broadcast_to(mean, (1, 128))
                means[d * 2 + h, c + 4 : c + 5, :] = jnp.broadcast_to(mean, (1, 128))
    sub = iota((8, wide), 0)
    part = iota((32, 512), 0)
    comp = iota((32, 512), 1) // 128
    coord = (part == comp) | (part == 8 + comp) | (part == 20 + comp)
    length = (part >= 24) & (part < 27)
    pick = ((comp < 3) & coord) | ((comp == 3) & length)
    pick = pick.astype(jnp.float32).astype(jnp.bfloat16)
    for k in range(pairs):
        b = tile_ref[0, k]
        t = tiles[b]
        target_ref[k] = t
        mean_ref[k] = means[b]
        norm = jnp.sum(t * t, axis=0, keepdims=True)
        t8 = jnp.where(sub < 4, t, jnp.concatenate([t[4:8], t[0:4]], axis=0))
        t8 = jnp.where(sub % 4 == 3, 1.0, t8)
        high, mid, low = split3(t8)
        nh, nm, nl = split3(norm)
        last = jnp.where(
            sub == 0, nh, jnp.where(sub == 1, nm, jnp.where(sub == 2, nl, 0.0))
        )
        stack = jnp.concatenate([high, mid, jnp.where(sub < 4, high, low), last], axis=0)
        feat_ref[k] = stack.T.astype(jnp.bfloat16)
        spread = jnp.dot(feat_ref[k], pick, preferred_element_type=jnp.float32)
        for c in range(4):
            wide_ref[k, c] = spread[:, c * 128 : (c + 1) * 128]
    for copy in copies[4:]:
        copy.wait()


def gather_tiles(values, mask_ref, b, rows):
    total = None
    for k in range(values.shape[0]):
        live = mask_ref[b, k : k + 1, :] > 0.5
        part = jnp.where(live, values[k, 0:rows, :], 0.0)
        total = part if total is None else total + part
    return total


def field_kernel(
    nodes,
    own_ref,
    side_ref,
    feats,
    targets,
    means,
    lanes_x,
    head_ref,
    base_ref,
    want_ref,
    mask_ref,
    applied_ref,
    up_ref,
    normal_ref,
    weight_ref,
    trac_ref,
    send_ref,
    cube_ref,
    hot_ref,
    fine_ref,
    block,
    values,
    field,
    src_a,
    src_b,
    coef_a,
    coef_b,
    row_a,
    row_b,
):
    pairs = values.shape[0]
    drops = weight_ref.shape[0]
    half = nodes // 2
    wide = feats.shape[1]
    fine_nodes = up_ref.shape[1]

    height = pairs * 4
    lane_id = iota((height, 128), 1)
    table = select(head_ref[...], own_ref, side_ref, nodes // 128 * 128)
    chosen = jnp.sum(
        jnp.where(lane_id == want_ref[...], table, 0.0), axis=1, keepdims=True
    )
    column = base_ref[...] + chosen.astype(jnp.int32)
    for i in range(3):
        hot = (lane_id + i * 128 == column).astype(jnp.float32)
        hot_ref[:, i * 128 : (i + 1) * 128] = hot.astype(jnp.bfloat16)
    picked = select(hot_ref[...], own_ref, side_ref, 0)
    fine = jnp.dot(
        picked[:, 0:nodes].astype(jnp.bfloat16),
        up_ref[...],
        preferred_element_type=jnp.float32,
    )
    for k in range(pairs):
        one = fine[k * 4 : (k + 1) * 4]
        fine_ref[k] = jnp.concatenate([one, one], axis=0)

    sub_f = iota((8, fine_nodes), 0)

    def prepare(k, src, coefs, qrow):
        f = fine_ref[k]
        charge = f[3:4]
        y = f - means[k, :, 0:1]
        y_only = jnp.where(sub_f < 3, y, 0.0)
        norm = jnp.sum(y_only * y_only, axis=0, keepdims=True) + REG
        q = jnp.where(sub_f % 4 == 3, norm, -2.0 * y)
        qrow[...] = q
        high, mid, low = split3(q)
        first = jnp.where(sub_f < 4, high, mid)
        second = jnp.where(sub_f < 4, low, high)
        third = jnp.where(sub_f < 3, 1.0, 0.0)
        src[...] = jnp.concatenate([first, first, second, third], axis=0).astype(jnp.bfloat16)
        coef = jnp.where(sub_f % 4 == 3, charge, charge * y)
        high, mid, low = split3(coef)
        coefs[...] = jnp.concatenate(
            [jnp.where(sub_f < 4, high, mid), jnp.where(sub_f < 4, low, 0.0)], axis=0
        ).astype(jnp.bfloat16)

    def work(k, src, coefs, qrow):
        tgt = feats[k]
        cubes = []
        for lo in range(0, fine_nodes, 256):
            hi = min(lo + 256, fine_nodes)
            if lo // 256 in VECTOR_CHUNKS:
                parts = []
                for at in range(lo, hi, 128):
                    end = min(at + 128, hi)
                    d = lanes_x[k, 3][:, : end - at] + qrow[3:4, at:end]
                    for c in range(3):
                        d = d + lanes_x[k, c][:, : end - at] * qrow[c : c + 1, at:end]
                    parts.append(inverse_cube(d))
                cube = jnp.concatenate(parts, axis=1) if len(parts) > 1 else parts[0]
            else:
                dist = jnp.dot(tgt, src[:, lo:hi], preferred_element_type=jnp.float32)
                cube = inverse_cube(dist)
            cube_ref[k, :, lo:hi] = cube
            cubes.append(cube)
        total = lax.dot_general(
            jnp.concatenate(cubes, axis=1),
            coefs[...],
            (((1,), (1,)), ((), ())),
            preferred_element_type=jnp.float32,
        )
        sums = total.T
        sums = sums[0:8] + sums[8:16]
        sums = sums + jnp.concatenate([sums[4:8], sums[0:4]], axis=0)
        values[k] = (targets[k] * sums[3:4] - sums) * (1.0 / (4.0 * math.pi))

    prepare(0, src_a, coef_a, row_a)

    def two(i, carry):
        k = 2 * i
        prepare(k + 1, src_b, coef_b, row_b)
        work(k, src_a, coef_a, row_a)
        prepare(jnp.minimum(k + 2, pairs - 1), src_a, coef_a, row_a)
        work(k + 1, src_b, coef_b, row_b)
        return carry

    lax.fori_loop(0, pairs // 2, two, 0)

    block[...] = jnp.zeros_like(block)
    for d in range(drops):
        for h, (lo, hi) in enumerate(tile_slices(nodes)):
            near = gather_tiles(values, mask_ref, d * 2 + h, 8)
            for c in range(3):
                field[c, d : d + 1, lo:hi] = near[c : c + 1, 0:half]
    e = [field[c] + applied_ref[c, :, 0:nodes] for c in range(3)]
    n = [normal_ref[c] for c in range(3)]
    along = e[0] * n[0] + e[1] * n[1] + e[2] * n[2]
    square = 0.5 * (e[0] * e[0] + e[1] * e[1] + e[2] * e[2])
    for c in range(3):
        t = along * e[c] - square * n[c]
        trac_ref[c] = t
        block[c * 4 : (c + 1) * 4, 0:nodes] = t * weight_ref[...]
    packed = block[...].astype(jnp.bfloat16)
    for i in range(send_ref.shape[0]):
        send_ref[i] = packed


def stokes_kernel(
    nodes,
    own_ref,
    side_ref,
    targets,
    means,
    mask_ref,
    up_ref,
    cube_ref,
    hot_ref,
    fine_ref,
    trac_ref,
    vel_ref,
    trac_hbm,
    forces,
    values,
    coef_a,
    coef_b,
    sems,
):
    copies = fetch_all([(trac_ref, trac_hbm)], sems)
    pairs = values.shape[0]
    drops = vel_ref.shape[1]
    half = nodes // 2
    fine_nodes = up_ref.shape[1]
    wide = targets.shape[2]

    picked = select(hot_ref[...], own_ref, side_ref, 0)
    fine = jnp.dot(
        picked[:, 0:nodes].astype(jnp.bfloat16),
        up_ref[...],
        preferred_element_type=jnp.float32,
    )
    for k in range(pairs):
        one = fine[k * 4 : (k + 1) * 4]
        forces[k] = jnp.concatenate([one, one], axis=0)

    sub_f = iota((8, fine_nodes), 0)

    def prepare(k, coefs):
        y = fine_ref[k] - means[k, :, 0:1]
        f = forces[k]
        y_only = jnp.where(sub_f < 3, y, 0.0)
        norm = jnp.sum(y_only * y_only, axis=0, keepdims=True)
        dot = jnp.sum(y_only * f, axis=0, keepdims=True)
        one = f * jnp.where(sub_f < 4, 1.0, norm)
        two = f * jnp.where(sub_f < 4, y[0:1], y[1:2])
        three = jnp.where(sub_f < 4, f * y[2:3], dot * y)
        parts = [split3(one), split3(two), split3(three)]
        coefs[...] = jnp.concatenate(
            [parts[g][s] for s in range(3) for g in range(3)]
            + [jnp.zeros((8, fine_nodes), jnp.float32)],
            axis=0,
        ).astype(jnp.bfloat16)

    def work(k, coefs):
        total = jnp.zeros((wide, 80), jnp.float32)
        for lo in range(0, fine_nodes, 256):
            hi = min(lo + 256, fine_nodes)
            total = total + lax.dot_general(
                cube_ref[k, :, lo:hi],
                coefs[:, lo:hi],
                (((1,), (1,)), ((), ())),
                preferred_element_type=jnp.float32,
            )
        sums = total.T
        sums = sums[0:24] + sums[24:48] + sums[48:72]
        x = targets[k][0:3]
        force, force_sq = sums[0:3], sums[4:7]
        t0, t1, t2 = sums[8:11], sums[12:15], sums[16:19]
        last = sums[20:23]
        x0, x1, x2 = x[0:1], x[1:2], x[2:3]
        square = x0 * x0 + x1 * x1 + x2 * x2
        trace = t0[0:1] + t1[1:2] + t2[2:3]
        reach = jnp.sum(x * force, axis=0, keepdims=True) - trace
        mixed = jnp.concatenate(
            [jnp.sum(x * t, axis=0, keepdims=True) for t in (t0, t1, t2)], axis=0
        )
        v = (square + 2.0 * REG) * force + force_sq
        v = v - 2.0 * (x0 * t0 + x1 * t1 + x2 * t2) + x * reach - mixed + last
        values[k, 0:3, :] = v * (1.0 / (8.0 * math.pi))

    prepare(0, coef_a)

    for k in range(pairs):
        if k + 1 < pairs:
            prepare(k + 1, coef_a if k % 2 else coef_b)
        work(k, coef_b if k % 2 else coef_a)
    for d in range(drops):
        for h, (lo, hi) in enumerate(tile_slices(nodes)):
            flow = gather_tiles(values, mask_ref, d * 2 + h, 3)
            for c in range(3):
                vel_ref[c, d : d + 1, lo:hi] = flow[c : c + 1, 0:half]
    copies[0].wait()


def exchange(mine, chips):
    own = lax.all_to_all(mine, ("core", "tgt"), 0, 0)
    moves = [(2 * i, 2 * i + 2) for i in range(chips - 1)]
    moves += [(2 * i + 3, 2 * i + 1) for i in range(chips - 1)]
    side = lax.ppermute(own, ("chip", "core"), moves)
    return own, side


def in_hbm(*arrays):
    return [pltpu.with_memory_space_constraint(a, pltpu.HBM) for a in arrays]


def share(side):
    return lax.all_gather(side, "core")


def local(
    chips,
    positions,
    normals,
    charge,
    weights,
    applied,
    upsample,
    send_list,
    send_count,
    pair_slot,
    pair_tile,
    pair_count,
):
    drops, _, nodes = positions.shape
    fine_nodes = upsample.shape[1]
    pairs = pair_slot.shape[2]
    lanes = ceil_to(nodes + 20, 128)
    wide = ceil_to(nodes // 2, 16)
    tiles = 2 * drops
    f32, bf16 = jnp.float32, jnp.bfloat16
    slots, tile_ids, count = pair_slot[0], pair_tile[0], pair_count

    positions = positions.transpose(1, 0, 2)
    normals = normals.transpose(1, 0, 2)

    i32 = jnp.int32
    dma = pltpu.SemaphoreType.DMA
    mine = pl.pallas_call(
        functools.partial(pack_kernel, nodes),
        out_shape=jax.ShapeDtypeStruct((8, 16, lanes), bf16),
        in_specs=[HBM] * 4,
        out_specs=VMEM,
        scratch_shapes=[
            pltpu.SMEM(send_list.shape[:1:-1], i32),
            pltpu.VMEM((3, drops, nodes), f32),
            pltpu.VMEM((drops, nodes), f32),
            pltpu.VMEM((drops, nodes), f32),
            pltpu.VMEM((16, lanes), f32),
            dma((4,)),
        ],
        compiler_params=pltpu.CompilerParams(vmem_limit_bytes=LIMIT[0]),
        name="pack",
    )(*in_hbm(send_list[0, 0].T, positions, charge, weights))
    own, side = exchange(mine, chips)

    shape = jax.ShapeDtypeStruct
    info = pl.pallas_call(
        target_kernel,
        out_shape=(
            shape((pairs, wide, 32), bf16),
            shape((pairs, 8, wide), f32),
            shape((pairs, 8, 128), f32),
            shape((pairs, 4, wide, 128), f32),
            shape((pairs * 4, 384), bf16),
            shape((pairs * 4, 128), i32),
            shape((pairs * 4, 128), i32),
            shape((tiles, pairs, wide), f32),
            shape((3, drops, lanes), f32),
            shape(upsample.shape, bf16),
            shape((3, drops, nodes), f32),
            shape((drops, nodes), f32),
        ),
        in_specs=[SMEM] + [HBM] * 7,
        out_specs=(VMEM,) * 12,
        scratch_shapes=[
            pltpu.VMEM((3, drops, nodes), f32),
            pltpu.SMEM((1, pairs), i32),
            pltpu.SMEM((1, pairs), i32),
            pltpu.SMEM((1, 3), f32),
            pltpu.VMEM((tiles, 8, wide), f32),
            pltpu.VMEM((tiles, 8, 128), f32),
            dma((7,)),
        ],
        compiler_params=pltpu.CompilerParams(vmem_limit_bytes=LIMIT[0]),
        cost_estimate=pl.CostEstimate(
            flops=4_000_000, bytes_accessed=6_000_000, transcendentals=0
        ),
        name="target",
    )(count, *in_hbm(positions, slots, tile_ids, applied[None], upsample, normals, weights))
    targets, means, mask, up = info[1], info[2], info[7], info[9]

    traction, forces, cubes, hot, fine = pl.pallas_call(
        functools.partial(field_kernel, nodes),
        out_shape=(
            shape((3, drops, nodes), f32),
            shape((8, 16, lanes), bf16),
            shape((pairs, wide, fine_nodes), bf16),
            shape((pairs * 4, 384), bf16),
            shape((pairs, 8, fine_nodes), f32),
        ),
        in_specs=[VMEM] * 14,
        out_specs=(VMEM,) * 5,
        scratch_shapes=[
            pltpu.VMEM((16, lanes), f32),
            pltpu.VMEM((pairs, 8, wide), f32),
            pltpu.VMEM((3, drops, nodes), f32),
            pltpu.VMEM((32, fine_nodes), bf16),
            pltpu.VMEM((32, fine_nodes), bf16),
            pltpu.VMEM((16, fine_nodes), bf16),
            pltpu.VMEM((16, fine_nodes), bf16),
            pltpu.VMEM((8, fine_nodes), f32),
            pltpu.VMEM((8, fine_nodes), f32),
        ],
        compiler_params=pltpu.CompilerParams(vmem_limit_bytes=LIMIT[1]),
        name="field",
    )(own, share(side), *info)
    own, side = exchange(forces, chips)

    velocity, traction = pl.pallas_call(
        functools.partial(stokes_kernel, nodes),
        out_shape=(shape((3, drops, nodes), f32),) * 2,
        in_specs=[VMEM] * 10,
        out_specs=(VMEM, HBM),
        scratch_shapes=[
            pltpu.VMEM((pairs, 8, fine_nodes), f32),
            pltpu.VMEM((pairs, 8, wide), f32),
            pltpu.VMEM((80, fine_nodes), bf16),
            pltpu.VMEM((80, fine_nodes), bf16),
            dma((1,)),
        ],
        compiler_params=pltpu.CompilerParams(vmem_limit_bytes=LIMIT[2]),
        name="stokes",
    )(own, share(side), targets, means, mask, up, cubes, hot, fine, traction)
    return traction.transpose(1, 0, 2), velocity.transpose(1, 0, 2)


def solution(mesh):
    space, tgt = mesh.shape["space"], mesh.shape["tgt"]
    chips = space // 2
    fine_mesh = Mesh(mesh.devices.reshape(chips, 2, tgt), ("chip", "core", "tgt"))
    every = ("chip", "core", "tgt")
    rows = ("chip", "core")
    placed = (
        P(every, None, None),
        P(every, None, None),
        P(every, None),
        P(every, None),
        P(),
        P(),
        P(rows, "tgt", None, None),
        P(rows, "tgt", None),
        P(rows, "tgt", None),
        P(rows, "tgt", None),
        P(rows, "tgt"),
    )
    return jax.shard_map(
        functools.partial(local, chips),
        mesh=fine_mesh,
        in_specs=placed,
        out_specs=(P(every, None, None), P(every, None, None)),
        check_vma=False,
    )
```

```python
import functools
import math

import jax
import jax.numpy as jnp
from jax import lax
from jax.experimental import pallas as pl
from jax.experimental.pallas import tpu as pltpu
from jax.sharding import Mesh
from jax.sharding import PartitionSpec as P

REG = 0.25
VMEM = pl.BlockSpec(memory_space=pltpu.VMEM)
HBM = pl.BlockSpec(memory_space=pltpu.HBM)
SMEM = pl.BlockSpec(memory_space=pltpu.SMEM)
VECTOR_CHUNKS = (7, 8)
LIMIT = (2 << 20, 20 << 20, 20 << 20)


def ceil_to(n, m):
    return -(-n // m) * m


def iota(shape, dim):
    return lax.broadcasted_iota(jnp.int32, shape, dim)


def split3(x):
    high = x.astype(jnp.bfloat16).astype(jnp.float32)
    rest = x - high
    mid = rest.astype(jnp.bfloat16).astype(jnp.float32)
    low = (rest - mid).astype(jnp.bfloat16).astype(jnp.float32)
    return high, mid, low


def fetch_all(pairs, sems):
    copies = [
        pltpu.make_async_copy(src, dst, sems.at[i]) for i, (src, dst) in enumerate(pairs)
    ]
    for copy in copies:
        copy.start()
    return copies


def pack_kernel(
    nodes, send_hbm, pos_hbm, charge_hbm, weight_hbm, out_ref,
    send_ref, pos_ref, charge_ref, weight_ref, block, sems,
):
    copies = fetch_all(
        [
            (send_hbm, send_ref),
            (pos_hbm, pos_ref),
            (charge_hbm, charge_ref),
            (weight_hbm, weight_ref),
        ],
        sems,
    )
    lanes = block.shape[1]
    block[...] = jnp.zeros_like(block)
    for copy in copies:
        copy.wait()
    for c in range(3):
        block[c * 4 : (c + 1) * 4, 0:nodes] = pos_ref[c]
    block[12:16, 0:nodes] = charge_ref[...] * weight_ref[...]
    base = nodes - (lanes - 128)
    lane = iota((1, 128), 1)
    row = block[0:1, lanes - 128 : lanes]
    slots, shell = send_ref.shape
    for o in range(shell):
        for j in range(slots):
            row = jnp.where(
                lane == base + o * slots + j, send_ref[j, o].astype(jnp.float32), row
            )
    block[0:1, lanes - 128 : lanes] = row
    packed = block[...].astype(jnp.bfloat16)
    for i in range(out_ref.shape[0]):
        out_ref[i] = packed


def block_index(p, core):
    place = core + 4 - (p // 4) % 5
    return ((place // 2) * 8 + (place % 2) * 4 + p // 20) * 16


def select(hot, own_ref, side_ref, lo):
    total = None
    for i, ref in enumerate((side_ref.at[0], own_ref, side_ref.at[1])):
        blocks = ref[...]
        blocks = blocks.reshape(blocks.shape[0] * blocks.shape[1], blocks.shape[2])
        part = jnp.dot(
            hot[:, i * 128 : (i + 1) * 128],
            blocks[:, lo:],
            preferred_element_type=jnp.float32,
        )
        total = part if total is None else total + part
    return total


def inverse_cube(d):
    d = jnp.maximum(d.astype(jnp.bfloat16), jnp.bfloat16(REG))
    return lax.rsqrt(d * d * d)


def tile_slices(nodes):
    half = nodes // 2
    return [(0, half), (half, nodes)]


def target_kernel(
    count_ref, pos_hbm, slot_hbm, tile_hbm, applied_hbm, up_hbm, normal_hbm, weight_hbm,
    feat_ref, target_ref, mean_ref, wide_ref, head_ref, base_ref, want_ref, mask_ref,
    applied_ref, up_ref, normal_ref, weight_ref,
    pos_ref, slot_ref, tile_ref, ambient_ref, tiles, means, sems,
):
    copies = fetch_all(
        [
            (pos_hbm, pos_ref),
            (slot_hbm, slot_ref),
            (tile_hbm, tile_ref),
            (applied_hbm, ambient_ref),
            (up_hbm, up_ref),
            (normal_hbm, normal_ref),
            (weight_hbm, weight_ref),
        ],
        sems,
    )
    for copy in copies[:4]:
        copy.wait()
    core = lax.axis_index("core")
    pairs = slot_ref.shape[1]
    drops, nodes = pos_ref.shape[1:]
    half = nodes // 2
    wide = feat_ref.shape[1]

    height = head_ref.shape[0]
    row = iota((height, 128), 0)
    start = jnp.zeros((height, 128), jnp.int32)
    want = jnp.zeros((height, 128), jnp.int32)
    for k in range(pairs):
        p = slot_ref[0, k]
        start = jnp.where(row // 4 == k, block_index(p, core), start)
        want = jnp.where(row // 4 == k, nodes % 128 + p % 20, want)
    lane = iota((height, 128), 1)
    base_ref[...] = start + (row % 4) * 4
    want_ref[...] = want
    for i in range(3):
        head = (lane + i * 128 == start).astype(jnp.float32)
        head_ref[:, i * 128 : (i + 1) * 128] = head.astype(jnp.bfloat16)

    for c in range(3):
        applied_ref[c] = jnp.full(applied_ref.shape[1:], ambient_ref[0, c], jnp.float32)
    pair_id = iota((pairs, wide), 0)
    owner = jnp.full((pairs, wide), -1, jnp.int32)
    for k in range(pairs):
        mine = jnp.where(k < count_ref[0, 0], tile_ref[0, k], -1)
        owner = jnp.where(pair_id == k, mine, owner)
    for b in range(2 * drops):
        mask_ref[b] = (owner == b).astype(jnp.float32)

    tiles[...] = jnp.zeros_like(tiles)
    means[...] = jnp.zeros_like(means)
    for d in range(drops):
        for h, (lo, hi) in enumerate(tile_slices(nodes)):
            for c in range(3):
                line = pos_ref[c, d : d + 1, lo:hi]
                mean = jnp.sum(line, axis=1, keepdims=True) / half
                tiles[d * 2 + h, c : c + 1, 0:half] = line - mean
                means[d * 2 + h, c : c + 1, :] = jnp.broadcast_to(mean, (1, 128))
                means[d * 2 + h, c + 4 : c + 5, :] = jnp.broadcast_to(mean, (1, 128))
    sub = iota((8, wide), 0)
    part = iota((32, 512), 0)
    comp = iota((32, 512), 1) // 128
    coord = (part == comp) | (part == 8 + comp) | (part == 20 + comp)
    length = (part >= 24) & (part < 27)
    pick = ((comp < 3) & coord) | ((comp == 3) & length)
    pick = pick.astype(jnp.float32).astype(jnp.bfloat16)
    for k in range(pairs):
        b = tile_ref[0, k]
        t = tiles[b]
        target_ref[k] = t
        mean_ref[k] = means[b]
        norm = jnp.sum(t * t, axis=0, keepdims=True)
        t8 = jnp.where(sub < 4, t, jnp.concatenate([t[4:8], t[0:4]], axis=0))
        t8 = jnp.where(sub % 4 == 3, 1.0, t8)
        high, mid, low = split3(t8)
        nh, nm, nl = split3(norm)
        last = jnp.where(
            sub == 0, nh, jnp.where(sub == 1, nm, jnp.where(sub == 2, nl, 0.0))
        )
        stack = jnp.concatenate([high, mid, jnp.where(sub < 4, high, low), last], axis=0)
        feat_ref[k] = stack.T.astype(jnp.bfloat16)
        spread = jnp.dot(feat_ref[k], pick, preferred_element_type=jnp.float32)
        for c in range(4):
            wide_ref[k, c] = spread[:, c * 128 : (c + 1) * 128]
    for copy in copies[4:]:
        copy.wait()


def gather_tiles(values, mask_ref, b, rows):
    total = None
    for k in range(values.shape[0]):
        live = mask_ref[b, k : k + 1, :] > 0.5
        part = jnp.where(live, values[k, 0:rows, :], 0.0)
        total = part if total is None else total + part
    return total


def field_kernel(
    nodes,
    own_ref,
    side_ref,
    feats,
    targets,
    means,
    lanes_x,
    head_ref,
    base_ref,
    want_ref,
    mask_ref,
    applied_ref,
    up_ref,
    normal_ref,
    weight_ref,
    trac_ref,
    send_ref,
    cube_ref,
    hot_ref,
    fine_ref,
    block,
    values,
    field,
    src_a,
    src_b,
    coef_a,
    coef_b,
    row_a,
    row_b,
):
    pairs = values.shape[0]
    drops = weight_ref.shape[0]
    half = nodes // 2
    wide = feats.shape[1]
    fine_nodes = up_ref.shape[1]

    height = pairs * 4
    lane_id = iota((height, 128), 1)
    table = select(head_ref[...], own_ref, side_ref, nodes // 128 * 128)
    chosen = jnp.sum(
        jnp.where(lane_id == want_ref[...], table, 0.0), axis=1, keepdims=True
    )
    column = base_ref[...] + chosen.astype(jnp.int32)
    for i in range(3):
        hot = (lane_id + i * 128 == column).astype(jnp.float32)
        hot_ref[:, i * 128 : (i + 1) * 128] = hot.astype(jnp.bfloat16)
    picked = select(hot_ref[...], own_ref, side_ref, 0)
    fine = jnp.dot(
        picked[:, 0:nodes].astype(jnp.bfloat16),
        up_ref[...],
        preferred_element_type=jnp.float32,
    )
    for k in range(pairs):
        one = fine[k * 4 : (k + 1) * 4]
        fine_ref[k] = jnp.concatenate([one, one], axis=0)

    sub_f = iota((8, fine_nodes), 0)

    def prepare(k, src, coefs, qrow):
        f = fine_ref[k]
        charge = f[3:4]
        y = f - means[k, :, 0:1]
        y_only = jnp.where(sub_f < 3, y, 0.0)
        norm = jnp.sum(y_only * y_only, axis=0, keepdims=True) + REG
        q = jnp.where(sub_f % 4 == 3, norm, -2.0 * y)
        qrow[...] = q
        high, mid, low = split3(q)
        first = jnp.where(sub_f < 4, high, mid)
        second = jnp.where(sub_f < 4, low, high)
        third = jnp.where(sub_f < 3, 1.0, 0.0)
        src[...] = jnp.concatenate([first, first, second, third], axis=0).astype(jnp.bfloat16)
        coef = jnp.where(sub_f % 4 == 3, charge, charge * y)
        high, mid, low = split3(coef)
        coefs[...] = jnp.concatenate(
            [jnp.where(sub_f < 4, high, mid), jnp.where(sub_f < 4, low, 0.0)], axis=0
        ).astype(jnp.bfloat16)

    def work(k, src, coefs, qrow):
        tgt = feats[k]
        cubes = []
        for lo in range(0, fine_nodes, 256):
            hi = min(lo + 256, fine_nodes)
            if lo // 256 in VECTOR_CHUNKS:
                parts = []
                for at in range(lo, hi, 128):
                    end = min(at + 128, hi)
                    d = lanes_x[k, 3][:, : end - at] + qrow[3:4, at:end]
                    for c in range(3):
                        d = d + lanes_x[k, c][:, : end - at] * qrow[c : c + 1, at:end]
                    parts.append(inverse_cube(d))
                cube = jnp.concatenate(parts, axis=1) if len(parts) > 1 else parts[0]
            else:
                dist = jnp.dot(tgt, src[:, lo:hi], preferred_element_type=jnp.float32)
                cube = inverse_cube(dist)
            cube_ref[k, :, lo:hi] = cube
            cubes.append(cube)
        total = lax.dot_general(
            jnp.concatenate(cubes, axis=1),
            coefs[...],
            (((1,), (1,)), ((), ())),
            preferred_element_type=jnp.float32,
        )
        sums = total.T
        sums = sums[0:8] + sums[8:16]
        sums = sums + jnp.concatenate([sums[4:8], sums[0:4]], axis=0)
        values[k] = (targets[k] * sums[3:4] - sums) * (1.0 / (4.0 * math.pi))

    prepare(0, src_a, coef_a, row_a)

    for k in range(pairs):
        if k + 1 < pairs:
            prepare(k + 1, *((src_a, coef_a, row_a) if k % 2 else (src_b, coef_b, row_b)))
        work(k, *((src_b, coef_b, row_b) if k % 2 else (src_a, coef_a, row_a)))

    block[...] = jnp.zeros_like(block)
    for d in range(drops):
        for h, (lo, hi) in enumerate(tile_slices(nodes)):
            near = gather_tiles(values, mask_ref, d * 2 + h, 8)
            for c in range(3):
                field[c, d : d + 1, lo:hi] = near[c : c + 1, 0:half]
    e = [field[c] + applied_ref[c, :, 0:nodes] for c in range(3)]
    n = [normal_ref[c] for c in range(3)]
    along = e[0] * n[0] + e[1] * n[1] + e[2] * n[2]
    square = 0.5 * (e[0] * e[0] + e[1] * e[1] + e[2] * e[2])
    for c in range(3):
        t = along * e[c] - square * n[c]
        trac_ref[c] = t
        block[c * 4 : (c + 1) * 4, 0:nodes] = t * weight_ref[...]
    packed = block[...].astype(jnp.bfloat16)
    for i in range(send_ref.shape[0]):
        send_ref[i] = packed


def stokes_kernel(
    nodes,
    own_ref,
    side_ref,
    targets,
    means,
    mask_ref,
    up_ref,
    cube_ref,
    hot_ref,
    fine_ref,
    trac_ref,
    vel_ref,
    trac_hbm,
    forces,
    values,
    coef_a,
    coef_b,
    sems,
):
    copies = fetch_all([(trac_ref, trac_hbm)], sems)
    pairs = values.shape[0]
    drops = vel_ref.shape[1]
    half = nodes // 2
    fine_nodes = up_ref.shape[1]
    wide = targets.shape[2]

    picked = select(hot_ref[...], own_ref, side_ref, 0)
    fine = jnp.dot(
        picked[:, 0:nodes].astype(jnp.bfloat16),
        up_ref[...],
        preferred_element_type=jnp.float32,
    )
    for k in range(pairs):
        one = fine[k * 4 : (k + 1) * 4]
        forces[k] = jnp.concatenate([one, one], axis=0)

    sub_f = iota((8, fine_nodes), 0)

    def prepare(k, coefs):
        y = fine_ref[k] - means[k, :, 0:1]
        f = forces[k]
        y_only = jnp.where(sub_f < 3, y, 0.0)
        norm = jnp.sum(y_only * y_only, axis=0, keepdims=True)
        dot = jnp.sum(y_only * f, axis=0, keepdims=True)
        one = f * jnp.where(sub_f < 4, 1.0, norm)
        two = f * jnp.where(sub_f < 4, y[0:1], y[1:2])
        three = jnp.where(sub_f < 4, f * y[2:3], dot * y)
        parts = [split3(one), split3(two), split3(three)]
        coefs[...] = jnp.concatenate(
            [parts[g][s] for s in range(3) for g in range(3)]
            + [jnp.zeros((8, fine_nodes), jnp.float32)],
            axis=0,
        ).astype(jnp.bfloat16)

    def work(k, coefs):
        total = jnp.zeros((wide, 80), jnp.float32)
        for lo in range(0, fine_nodes, 256):
            hi = min(lo + 256, fine_nodes)
            total = total + lax.dot_general(
                cube_ref[k, :, lo:hi],
                coefs[:, lo:hi],
                (((1,), (1,)), ((), ())),
                preferred_element_type=jnp.float32,
            )
        sums = total.T
        sums = sums[0:24] + sums[24:48] + sums[48:72]
        x = targets[k][0:3]
        force, force_sq = sums[0:3], sums[4:7]
        t0, t1, t2 = sums[8:11], sums[12:15], sums[16:19]
        last = sums[20:23]
        x0, x1, x2 = x[0:1], x[1:2], x[2:3]
        square = x0 * x0 + x1 * x1 + x2 * x2
        trace = t0[0:1] + t1[1:2] + t2[2:3]
        reach = jnp.sum(x * force, axis=0, keepdims=True) - trace
        mixed = jnp.concatenate(
            [jnp.sum(x * t, axis=0, keepdims=True) for t in (t0, t1, t2)], axis=0
        )
        v = (square + 2.0 * REG) * force + force_sq
        v = v - 2.0 * (x0 * t0 + x1 * t1 + x2 * t2) + x * reach - mixed + last
        values[k, 0:3, :] = v * (1.0 / (8.0 * math.pi))

    prepare(0, coef_a)

    for k in range(pairs):
        if k + 1 < pairs:
            prepare(k + 1, coef_a if k % 2 else coef_b)
        work(k, coef_b if k % 2 else coef_a)
    for d in range(drops):
        for h, (lo, hi) in enumerate(tile_slices(nodes)):
            flow = gather_tiles(values, mask_ref, d * 2 + h, 3)
            for c in range(3):
                vel_ref[c, d : d + 1, lo:hi] = flow[c : c + 1, 0:half]
    copies[0].wait()


def exchange(mine, chips):
    own = lax.all_to_all(mine, ("core", "tgt"), 0, 0)
    moves = [(2 * i, 2 * i + 2) for i in range(chips - 1)]
    moves += [(2 * i + 3, 2 * i + 1) for i in range(chips - 1)]
    side = lax.ppermute(own, ("chip", "core"), moves)
    return own, side


def in_hbm(*arrays):
    return [pltpu.with_memory_space_constraint(a, pltpu.HBM) for a in arrays]


def share(side):
    return lax.all_gather(side, "core")


def local(
    chips,
    positions,
    normals,
    charge,
    weights,
    applied,
    upsample,
    send_list,
    send_count,
    pair_slot,
    pair_tile,
    pair_count,
):
    drops, _, nodes = positions.shape
    fine_nodes = upsample.shape[1]
    pairs = pair_slot.shape[2]
    lanes = ceil_to(nodes + 20, 128)
    wide = ceil_to(nodes // 2, 16)
    tiles = 2 * drops
    f32, bf16 = jnp.float32, jnp.bfloat16
    slots, tile_ids, count = pair_slot[0], pair_tile[0], pair_count

    positions = positions.transpose(1, 0, 2)
    normals = normals.transpose(1, 0, 2)

    i32 = jnp.int32
    dma = pltpu.SemaphoreType.DMA
    mine = pl.pallas_call(
        functools.partial(pack_kernel, nodes),
        out_shape=jax.ShapeDtypeStruct((8, 16, lanes), bf16),
        in_specs=[HBM] * 4,
        out_specs=VMEM,
        scratch_shapes=[
            pltpu.SMEM(send_list.shape[:1:-1], i32),
            pltpu.VMEM((3, drops, nodes), f32),
            pltpu.VMEM((drops, nodes), f32),
            pltpu.VMEM((drops, nodes), f32),
            pltpu.VMEM((16, lanes), f32),
            dma((4,)),
        ],
        compiler_params=pltpu.CompilerParams(vmem_limit_bytes=LIMIT[0]),
        name="pack",
    )(*in_hbm(send_list[0, 0].T, positions, charge, weights))
    own, side = exchange(mine, chips)

    shape = jax.ShapeDtypeStruct
    info = pl.pallas_call(
        target_kernel,
        out_shape=(
            shape((pairs, wide, 32), bf16),
            shape((pairs, 8, wide), f32),
            shape((pairs, 8, 128), f32),
            shape((pairs, 4, wide, 128), f32),
            shape((pairs * 4, 384), bf16),
            shape((pairs * 4, 128), i32),
            shape((pairs * 4, 128), i32),
            shape((tiles, pairs, wide), f32),
            shape((3, drops, lanes), f32),
            shape(upsample.shape, bf16),
            shape((3, drops, nodes), f32),
            shape((drops, nodes), f32),
        ),
        in_specs=[SMEM] + [HBM] * 7,
        out_specs=(VMEM,) * 12,
        scratch_shapes=[
            pltpu.VMEM((3, drops, nodes), f32),
            pltpu.SMEM((1, pairs), i32),
            pltpu.SMEM((1, pairs), i32),
            pltpu.SMEM((1, 3), f32),
            pltpu.VMEM((tiles, 8, wide), f32),
            pltpu.VMEM((tiles, 8, 128), f32),
            dma((7,)),
        ],
        compiler_params=pltpu.CompilerParams(vmem_limit_bytes=LIMIT[0]),
        cost_estimate=pl.CostEstimate(
            flops=4_000_000, bytes_accessed=6_000_000, transcendentals=0
        ),
        name="target",
    )(count, *in_hbm(positions, slots, tile_ids, applied[None], upsample, normals, weights))
    targets, means, mask, up = info[1], info[2], info[7], info[9]

    traction, forces, cubes, hot, fine = pl.pallas_call(
        functools.partial(field_kernel, nodes),
        out_shape=(
            shape((3, drops, nodes), f32),
            shape((8, 16, lanes), bf16),
            shape((pairs, wide, fine_nodes), bf16),
            shape((pairs * 4, 384), bf16),
            shape((pairs, 8, fine_nodes), f32),
        ),
        in_specs=[VMEM] * 14,
        out_specs=(VMEM,) * 5,
        scratch_shapes=[
            pltpu.VMEM((16, lanes), f32),
            pltpu.VMEM((pairs, 8, wide), f32),
            pltpu.VMEM((3, drops, nodes), f32),
            pltpu.VMEM((32, fine_nodes), bf16),
            pltpu.VMEM((32, fine_nodes), bf16),
            pltpu.VMEM((16, fine_nodes), bf16),
            pltpu.VMEM((16, fine_nodes), bf16),
            pltpu.VMEM((8, fine_nodes), f32),
            pltpu.VMEM((8, fine_nodes), f32),
        ],
        compiler_params=pltpu.CompilerParams(vmem_limit_bytes=LIMIT[1]),
        name="field",
    )(own, share(side), *info)
    own, side = exchange(forces, chips)

    velocity, traction = pl.pallas_call(
        functools.partial(stokes_kernel, nodes),
        out_shape=(shape((3, drops, nodes), f32),) * 2,
        in_specs=[VMEM] * 10,
        out_specs=(VMEM, HBM),
        scratch_shapes=[
            pltpu.VMEM((pairs, 8, fine_nodes), f32),
            pltpu.VMEM((pairs, 8, wide), f32),
            pltpu.VMEM((80, fine_nodes), bf16),
            pltpu.VMEM((80, fine_nodes), bf16),
            dma((1,)),
        ],
        compiler_params=pltpu.CompilerParams(vmem_limit_bytes=LIMIT[2]),
        name="stokes",
    )(own, share(side), targets, means, mask, up, cubes, hot, fine, traction)
    return traction.transpose(1, 0, 2), velocity.transpose(1, 0, 2)


def solution(mesh):
    space, tgt = mesh.shape["space"], mesh.shape["tgt"]
    chips = space // 2
    fine_mesh = Mesh(mesh.devices.reshape(chips, 2, tgt), ("chip", "core", "tgt"))
    every = ("chip", "core", "tgt")
    rows = ("chip", "core")
    placed = (
        P(every, None, None),
        P(every, None, None),
        P(every, None),
        P(every, None),
        P(),
        P(),
        P(rows, "tgt", None, None),
        P(rows, "tgt", None),
        P(rows, "tgt", None),
        P(rows, "tgt", None),
        P(rows, "tgt"),
    )
    return jax.shard_map(
        functools.partial(local, chips),
        mesh=fine_mesh,
        in_specs=placed,
        out_specs=(P(every, None, None), P(every, None, None)),
        check_vma=False,
    )
```
